32 devices in a mesh: grp: 4 (over y, x), tile: 8 (over z, core).
Axes of the slice: x: 2, y: 2, z: 4, core: 2. Of those that a mesh axis runs over, the one named last changes fastest.
Arguments:
- temp: bfloat16 [48, 64, 2048], P(None, 'grp', 'tile'), may hold values from -6 to 6
- humid: bfloat16 [48, 64, 2048], P(None, 'grp', 'tile'), may hold values from -5 to 5
- parent: int32 [64, 2048], P('grp', 'tile'), may hold values from 0 to 8191, as said below
- kabs: float32 [112, 48], replicated, may hold values from 0.003 to 1
- planck: float32 [112], replicated, may hold values from 0.5 to 2
- top_flux: float32 [112], replicated, may hold values from 0 to 2
Outputs:
- temp_next: bfloat16 [48, 64, 2048], P(None, 'grp', 'tile')
The draws below stay inside these ranges and needn't reach their ends.
Inputs may be any that keep to these rules, and one draw needn't show every extreme that they name: parent // 1024 is the tile index, in the same region, of the device owning that parent column; the fine cells of one device name any one owner at most 1024 times.
All inputs are finite; a program needn't handle non-finite values.
Results may differ from the reference program's by a relative error of at most 0.005.
Values may be sent and summed in bfloat16 or wider, within the bound.
A program may use at most 64 MiB of HBM per device.

```python
import math
import jax
import jax.numpy as jnp
from jax import lax

NLEV = 48
G = 112
FR = 16
FCOL = 256
CC = 1024
NCO = 8192
NY = 64
NX = 2048
N_GRP = 4
N_TILE = 8


def draw_parent(key, part):
    fine = FR * FCOL
    assigned_slots = 2 * fine
    capacity_limit = assigned_slots // N_TILE
    owned = fine // 4
    keys = jax.random.split(jax.random.fold_in(key, 17), 4)
    rank_keys = jax.random.split(keys[0], N_GRP)
    hot_rank = jax.vmap(lambda k: jax.random.permutation(k, N_TILE))(rank_keys)
    busiest_flag = (hot_rank < max(N_TILE // 4, 1)).astype(jnp.int32)
    random_jitter = jax.random.randint(keys[1], (N_GRP, N_TILE, assigned_slots), 0, 512)
    slot_numbers = jnp.arange(assigned_slots, dtype=jnp.int32)
    extra_priority = busiest_flag[:, slot_numbers // capacity_limit]
    ranking_score = (random_jitter + 512 * extra_priority[:, None, :]) * assigned_slots + slot_numbers[None, None, :]
    unused, chosen = lax.top_k(ranking_score, fine)
    chosen = jax.random.permutation(keys[2], chosen, axis=2, independent=True)
    owner = chosen // capacity_limit
    local = jax.random.randint(keys[3], (N_GRP, N_TILE, fine), 0, owned)
    parent = (owner * owned + local).astype(jnp.int32)
    parent = parent.reshape(N_GRP, N_TILE, FR, FCOL)
    return jnp.transpose(parent, (0, 2, 1, 3)).reshape(N_GRP * FR, N_TILE * FCOL)


def block_levels(own_key, shape, cuts, smallest, high):
    loudness = 1.0
    for dim, shards_of in cuts:
        heights = jax.random.uniform(jax.random.fold_in(jax.random.fold_in(own_key, 6), dim), (shards_of,), jnp.float32, smallest / len(cuts), high / len(cuts))
        loudness = loudness * jnp.repeat(jnp.exp(heights), shape[dim] // shards_of).reshape((-1,) + (1,) * (len(shape) - 1 - dim))
    return loudness


def gaussian(key, extent, width, limit, cuts=(), kind=jnp.bfloat16):
    drawn = width * jax.random.normal(key, extent, jnp.float32)
    if cuts:
        drawn = drawn * block_levels(key, extent, cuts, -0.22, 0.18)
    return jnp.clip(drawn, -limit, limit).astype(kind)


def setup_inputs(seed: int = 0) -> dict:
    seeds = jax.random.split(jax.random.key(seed), 7)
    return {
        "temp": gaussian(seeds[0], (NLEV, NY, NX), 1.0, 6.0, ((1, 4), (2, 8))),
        "humid": gaussian(seeds[1], (NLEV, NY, NX), 1.0, 5.0, ((1, 4), (2, 8))),
        "parent": draw_parent(jax.random.fold_in(seeds[6], 71), 0),
        "kabs": jnp.clip(jnp.exp(jax.random.uniform(seeds[3], (G, NLEV), jnp.float32, math.log(0.003), math.log(1.0))), 0.003, 1.0),
        "planck": jnp.clip(jnp.exp(jax.random.uniform(seeds[4], (G,), jnp.float32, math.log(0.5), math.log(2.0))), 0.5, 2.0),
        "top_flux": jnp.clip(jax.random.uniform(seeds[5], (G,), jnp.float32, 0.0, 2.0), 0.0, 2.0),
    }


def recur(coef, source, init):
    levels = coef.shape[0]
    blocks = levels // 8
    rest = coef.shape[1:]
    coef4 = coef.reshape((blocks, 8) + rest)
    source4 = source.reshape((blocks, 8) + rest)
    prod_list = []
    part_list = []
    prod_now = jnp.ones((blocks,) + rest, jnp.float32)
    part_now = jnp.zeros((blocks,) + rest, jnp.float32)
    for inner in range(8):
        prod_now = coef4[:, inner] * prod_now
        part_now = coef4[:, inner] * part_now + source4[:, inner]
        prod_list.append(prod_now)
        part_list.append(part_now)
    starts = []
    carry = init
    for outer in range(blocks):
        starts.append(carry)
        carry = prod_list[7][outer] * carry + part_list[7][outer]
    start = jnp.stack(starts, 0)
    result = jnp.stack([prod_list[j] * start + part_list[j] for j in range(8)], 1)
    return result.reshape((levels,) + rest)


def radiate(tc, hc, kabs, planck, top_flux):
    levels, count = tc.shape
    kblk = kabs.reshape(-1, 16, levels)
    pblk = planck.reshape(-1, 16)
    tblk = top_flux.reshape(-1, 16)
    absorb = jnp.exp(0.5 * hc)[:, None, :]
    emit = jnp.exp(0.25 * tc)[:, None, :]

    def one_block(items):
        k_blk, p_blk, t_blk = items
        tau = jnp.transpose(k_blk)[:, :, None] * absorb
        trans = jnp.exp(-tau)
        source = p_blk[None, :, None] * emit * (1.0 - trans)
        top = jnp.broadcast_to(t_blk[:, None], (16, count)).astype(jnp.float32)
        down = recur(trans, source, top)
        up = recur(trans[::-1], source[::-1], 0.3 * down[-1])[::-1]
        net = down - up
        top_net = top - up[0]
        before = jnp.concatenate([top_net[None], net[:-1]], 0)
        return jnp.sum(before - net, axis=1)

    parts = lax.map(one_block, (kblk, pblk, tblk))
    return jnp.sum(parts, axis=0) * (levels / kabs.shape[0])


def laplace(field):
    value = field.astype(jnp.float32)
    return (jnp.roll(value, 1, 1) + jnp.roll(value, -1, 1) + jnp.roll(value, 1, 2) + jnp.roll(value, -1, 2) - 4.0 * value)


def reference(temp, humid, parent, kabs, planck, top_flux):
    levels = temp.shape[0]
    first = (temp.astype(jnp.float32) + 0.2 * laplace(temp)).astype(jnp.bfloat16)
    region = (jnp.arange(NY) // FR).astype(jnp.int32)
    global_id = (region[:, None] * NCO + parent).reshape(-1)
    total = N_GRP * NCO
    values = jnp.concatenate([temp.reshape(levels, -1), humid.reshape(levels, -1)], 0).astype(jnp.float32)
    sums = jax.ops.segment_sum(jnp.transpose(values), global_id, num_segments=total)
    counts = jax.ops.segment_sum(jnp.ones(global_id.shape, jnp.float32), global_id, num_segments=total)
    means = sums / jnp.maximum(counts, 1.0)[:, None]
    blocks = means.reshape(total // CC, CC, 2 * levels)

    def per_owner(block):
        tc = jnp.transpose(block[:, :levels])
        hc = jnp.transpose(block[:, levels:])
        return radiate(tc, hc, kabs, planck, top_flux)

    heat = lax.map(per_owner, blocks)
    heat_c = jnp.transpose(heat, (1, 0, 2)).reshape(levels, total).astype(jnp.bfloat16)
    hmean = jnp.transpose(means[:, levels:]).astype(jnp.bfloat16)
    heat_f = heat_c[:, global_id].astype(jnp.float32) + 0.5 * (humid.reshape(levels, -1).astype(jnp.float32) - hmean[:, global_id].astype(jnp.float32))
    second = (first.astype(jnp.float32) + 0.5 * heat_f.reshape(temp.shape)).astype(jnp.bfloat16)
    return (second.astype(jnp.float32) + 0.2 * laplace(second)).astype(jnp.bfloat16)
```

```python
import functools
import math

import jax
import jax.numpy as jnp
from jax import lax
from jax.experimental import pallas as pl
from jax.experimental.pallas import tpu as pltpu
from jax.sharding import PartitionSpec as P

F32 = jnp.float32
BF16 = jnp.bfloat16
VMEM_LIMIT = 60 * 1024 * 1024
VSPEC = pl.BlockSpec(memory_space=pltpu.VMEM)


def partial_kernel(chunks, offset_ref, temp_ref, humid_ref, parent_ref, out_ref, onehot, masked):
    rows, levels, lanes = temp_ref.shape
    step = pl.program_id(0)
    owner = 2 * step + offset_ref[0]
    data = 2 * levels * chunks
    row = lax.broadcasted_iota(jnp.int32, (16, lanes), 0)

    @pl.when(step == 0)
    def _():
        lo_iota = lax.broadcasted_iota(jnp.int32, (lanes, lanes), 0)
        for r in range(rows):
            low = parent_ref[r : r + 1, :] % lanes
            onehot[:, r * lanes : (r + 1) * lanes] = (lo_iota == low).astype(F32).astype(BF16)

    for r in range(rows):
        high = jnp.broadcast_to(parent_ref[r : r + 1, :] // lanes, (16, lanes))
        part = slice(r * lanes, (r + 1) * lanes)
        for c in range(chunks):
            mask = (high == owner * chunks + c).astype(F32).astype(BF16)
            for v in range(levels // 16):
                src = slice(v * 16, (v + 1) * 16)
                at = c * 2 * levels + v * 16
                masked[at : at + 16, part] = temp_ref[r, src, :] * mask
                masked[at + levels : at + levels + 16, part] = humid_ref[r, src, :] * mask
        masked[data : data + 16, part] = (high == owner * chunks + row // 2).astype(F32).astype(BF16)
    total = lax.dot_general(
        masked[...], onehot[...], (((1,), (1,)), ((), ())), preferred_element_type=F32
    )
    out_ref[0, :data, :] = total[:data].astype(out_ref.dtype)
    count = total[data:]
    high = jnp.floor(count * (1.0 / 32.0))
    out_ref[0, data:, :] = jnp.where(row % 2 == 0, high, count - 32.0 * high).astype(out_ref.dtype)


def radiate_kernel(levels, feats, recv_ref, kabs_in, planck_ref, top_ref, out_ref, kabs_ref, sums, absorb, emit, trans, net, heat):
    tiles = recv_ref.shape[0]
    lanes = recv_ref.shape[2]
    chunks = recv_ref.shape[1] // feats
    octets = kabs_in.shape[0] // 8
    group = octets // 2 if octets % 2 == 0 else octets
    width = 128
    data = chunks * feats
    for k in range(levels):
        kabs_ref[k] = jnp.broadcast_to(kabs_in[:, k : k + 1], kabs_ref.shape[1:])

    def add(i, carry):
        at = pl.ds(pl.multiple_of(i * 16, 16), 16)
        acc = recv_ref[0, at, :].astype(F32)
        for s in range(1, tiles):
            acc = acc + recv_ref[s, at, :].astype(F32)
        sums[at, :] = acc
        return carry

    lax.fori_loop(0, data // 16 + 1, add, 0)
    for c in range(chunks):
        base = c * feats
        cnt = sums[data + 2 * c : data + 2 * c + 1, :] * 32.0
        cnt = cnt + sums[data + 2 * c + 1 : data + 2 * c + 2, :]
        cnt = jnp.maximum(cnt, 1.0)
        for j in range(lanes // width):
            part = slice(j * width, (j + 1) * width)
            ct = c * (lanes // width) + j
            tc = sums[base : base + levels, part] / cnt[:, part]
            hc = sums[base + levels : base + 2 * levels, part] / cnt[:, part]
            emit[ct] = jnp.exp(0.25 * tc)
            absorb[ct] = jnp.exp(0.5 * hc) * (-math.log2(math.e))
            heat[ct] = -0.5 * hc

    scale = levels / (octets * 8)

    def column(ct, carry):
        for half in range(octets // group):
            gs = [(half * group + p) * 8 for p in range(group)]
            planck = [jnp.broadcast_to(planck_ref[g : g + 8, :], (8, width)) for g in gs]
            down = [jnp.broadcast_to(top_ref[g : g + 8, :], (8, width)) for g in gs]
            if half == 0:
                before = sum(down[1:], down[0])
                net[0] = before
            else:
                net[0] = net[0] + sum(down[1:], down[0])
            for k in range(levels):
                ab = absorb[ct, k : k + 1, :]
                em = emit[ct, k : k + 1, :]
                acc = None
                for p in range(group):
                    t = jnp.exp2(kabs_ref[k, gs[p] : gs[p] + 8, :] * ab)
                    trans[k, p] = t
                    s = planck[p] * em
                    down[p] = s + t * (down[p] - s)
                    acc = down[p] if acc is None else acc + down[p]
                net[k + 1] = acc if half == 0 else net[k + 1] + acc
            up = [0.3 * d for d in down]
            for k in range(levels - 1, -1, -1):
                em = emit[ct, k : k + 1, :]
                acc = None
                for p in range(group):
                    s = planck[p] * em
                    up[p] = s + trans[k, p] * (up[p] - s)
                    acc = up[p] if acc is None else acc + up[p]
                net[k + 1] = net[k + 1] - acc
            net[0] = net[0] - acc
        for k in range(levels):
            row = jnp.sum(net[k] - net[k + 1], axis=0, keepdims=True) * scale
            heat[ct, k : k + 1, :] = heat[ct, k : k + 1, :] + row
        return carry

    lax.fori_loop(0, chunks * lanes // width, column, 0)
    per = lanes // width
    for c in range(chunks):
        for j in range(per):
            out_ref[c * levels : (c + 1) * levels, j * width : (j + 1) * width] = heat[c * per + j].astype(BF16)


def laplace_row(centre, above, below, left, right):
    lanes = centre.shape[1]
    lane = lax.broadcasted_iota(jnp.int32, centre.shape, 1)
    west = jnp.where(lane == 0, left, pltpu.roll(centre, 1, 1))
    east = jnp.where(lane == lanes - 1, right, pltpu.roll(centre, lanes - 1, 1))
    return above + below + west + east - 4.0 * centre


def gather_kernel(levels, table_ref, parent_ref, temp_ref, humid_ref, up_ref, dn_ref, lf_ref, rt_ref, out_ref):
    rows, _, lanes = temp_ref.shape
    tiles = table_ref.shape[0]
    chunks = table_ref.shape[1] // levels
    lo_iota = lax.broadcasted_iota(jnp.int32, (lanes, lanes), 0)
    for r in range(rows):
        low = parent_ref[r : r + 1, :] % lanes
        high = jnp.broadcast_to(parent_ref[r : r + 1, :] // lanes, (levels, lanes))
        onehot = (lo_iota == low).astype(F32).astype(BF16)

        def owner(i, acc):
            span = 4
            got = jnp.dot(
                table_ref[pl.ds(i * span, span)].reshape(span * chunks * levels, lanes),
                onehot,
                preferred_element_type=F32,
            )
            for c in range(span * chunks):
                acc = jnp.where(high == i * span * chunks + c, got[c * levels : (c + 1) * levels], acc)
            return acc

        picked = lax.fori_loop(0, tiles // 4, owner, jnp.zeros((levels, lanes), F32))
        centre = temp_ref[r].astype(F32)
        above = (temp_ref[r - 1] if r > 0 else up_ref[0]).astype(F32)
        below = (temp_ref[r + 1] if r < rows - 1 else dn_ref[0]).astype(F32)
        lap = laplace_row(centre, above, below, lf_ref[:, r : r + 1], rt_ref[:, r : r + 1])
        first = (centre + 0.2 * lap).astype(BF16).astype(F32)
        heat_f = picked + 0.5 * humid_ref[r].astype(F32)
        out_ref[r] = (first + 0.5 * heat_f).astype(BF16)


def laplace_kernel(x_ref, up_ref, dn_ref, lf_ref, rt_ref, out_ref):
    rows = x_ref.shape[0]
    for r in range(rows):
        centre = x_ref[r].astype(F32)
        above = (x_ref[r - 1] if r > 0 else up_ref[0]).astype(F32)
        below = (x_ref[r + 1] if r < rows - 1 else dn_ref[0]).astype(F32)
        lap = laplace_row(centre, above, below, lf_ref[:, r : r + 1], rt_ref[:, r : r + 1])
        out_ref[r] = (centre + 0.2 * lap).astype(BF16)


def halos(x):
    g, t = lax.axis_size("grp"), lax.axis_size("tile")
    ahead = lambda n: [(i, (i + 1) % n) for i in range(n)]
    back = lambda n: [((i + 1) % n, i) for i in range(n)]
    up = lax.ppermute(x[-1:], "grp", ahead(g))
    dn = lax.ppermute(x[:1], "grp", back(g))
    lf = lax.ppermute(jnp.transpose(x[:, :, -1]), "tile", ahead(t)).astype(F32)
    rt = lax.ppermute(jnp.transpose(x[:, :, 0]), "tile", back(t)).astype(F32)
    return up, dn, lf, rt


def on_device(temp, humid, parent, kabs, planck, top_flux):
    levels, rows, lanes = temp.shape
    tiles = lax.axis_size("tile")
    owned = rows * lanes // 4
    chunks = owned // lanes
    feats = 2 * levels
    gpts = kabs.shape[0]
    params = pltpu.CompilerParams(vmem_limit_bytes=VMEM_LIMIT)

    x = jnp.transpose(temp, (1, 0, 2))
    h = jnp.transpose(humid, (1, 0, 2))
    size = chunks * feats + 16
    core = lax.rem(lax.axis_index("tile"), 2)
    half = tiles // 2

    def partial_sums(offset, dtype):
        return pl.pallas_call(
            functools.partial(partial_kernel, chunks),
            out_shape=jax.ShapeDtypeStruct((half, size, lanes), dtype),
            grid=(half,),
            in_specs=[
                pl.BlockSpec(memory_space=pltpu.SMEM),
                pl.BlockSpec((rows, levels, lanes), lambda i: (0, 0, 0)),
                pl.BlockSpec((rows, levels, lanes), lambda i: (0, 0, 0)),
                pl.BlockSpec((rows, lanes), lambda i: (0, 0)),
            ],
            out_specs=pl.BlockSpec((1, size, lanes), lambda i: (i, 0, 0)),
            scratch_shapes=[
                pltpu.VMEM((lanes, rows * lanes), BF16),
                pltpu.VMEM((size, rows * lanes), BF16),
            ],
            compiler_params=params,
            cost_estimate=pl.CostEstimate(
                flops=2 * half * size * rows * lanes * lanes,
                bytes_accessed=4 * half * size * lanes,
                transcendentals=0,
            ),
        )(offset.reshape(1).astype(jnp.int32), x, h, parent)

    theirs = partial_sums(1 - core, BF16)
    given = lax.ppermute(theirs, "tile", [(i, i ^ 1) for i in range(tiles)])
    mine = partial_sums(core, F32)
    partial = (mine + given.astype(F32)).astype(BF16)
    groups = [list(range(c, tiles, 2)) for c in range(2)]
    recv = lax.all_to_all(
        partial, "tile", split_axis=0, concat_axis=0, tiled=True, axis_index_groups=groups
    )

    ctiles = owned // 128
    octets = gpts // 8
    group = octets // 2 if octets % 2 == 0 else octets
    table = pl.pallas_call(
        functools.partial(radiate_kernel, levels, feats),
        out_shape=jax.ShapeDtypeStruct((chunks * levels, lanes), BF16),
        in_specs=[VSPEC] * 4,
        out_specs=VSPEC,
        scratch_shapes=[
            pltpu.VMEM((levels, gpts, 128), F32),
            pltpu.VMEM((size, lanes), F32),
            pltpu.VMEM((ctiles, levels, 128), F32),
            pltpu.VMEM((ctiles, levels, 128), F32),
            pltpu.VMEM((levels, group, 8, 128), F32),
            pltpu.VMEM((levels + 1, 8, 128), F32),
            pltpu.VMEM((ctiles, levels, 128), F32),
        ],
        compiler_params=params,
    )(recv, kabs, planck[:, None], top_flux[:, None])
    tables = lax.all_gather(table, "tile", axis=0)

    second = pl.pallas_call(
        functools.partial(gather_kernel, levels),
        out_shape=jax.ShapeDtypeStruct((rows, levels, lanes), BF16),
        in_specs=[VSPEC] * 8,
        out_specs=VSPEC,
        compiler_params=params,
    )(tables, parent, x, h, *halos(x))
    out = pl.pallas_call(
        laplace_kernel,
        out_shape=jax.ShapeDtypeStruct((rows, levels, lanes), BF16),
        in_specs=[VSPEC] * 5,
        out_specs=VSPEC,
        compiler_params=params,
    )(second, *halos(second))
    return jnp.transpose(out, (1, 0, 2))


class Layout:
    def __init__(self, tiles, levels, rows, lanes, gpts):
        self.tiles, self.levels, self.rows, self.lanes, self.gpts = tiles, levels, rows, lanes, gpts
        self.bits = tiles.bit_length() - 1
        self.owned = rows * lanes // 4
        self.chunks = self.owned // lanes
        self.feats = 2 * levels
        self.cells = rows * lanes
        order = [0]
        for b in reversed(range(self.bits)):
            order = order + [s ^ (1 << b) for s in order]
        self.order = order
        self.half = tiles // 2
        self.block = self.half * self.feats + 16

    def message(self, b):
        return (self.tiles >> (b + 1)) * self.feats + 16


def fused_fits(tiles, levels, rows, lanes, gpts):
    if tiles & (tiles - 1) or tiles < 4 or tiles > 16:
        return False
    if levels % 16 or lanes != 256 or rows % 16 or gpts % 8:
        return False
    lay = Layout(tiles, levels, rows, lanes, gpts)
    big = 2 * (2 * lay.block + lay.owned) * lay.cells
    return big <= VMEM_LIMIT // 2


def fused_kernel(lay, *refs):
    (temp_in, humid_in, parent_ref, kabs_in, planck_in, top_in, out_ref,
     raw, wide, x, h, onehot, masked, keep, *rest) = refs
    inb, rest = rest[: lay.bits], rest[lay.bits :]
    outb, rest = rest[: lay.bits], rest[lay.bits :]
    (tables, kabs, gvec, trans, net, emit, absorb, heat, sec, edge_out, edge_in, row_in,
     in_sem, stage_send, stage_recv, tab_send, tab_recv, halo_send, halo_recv) = rest
    L, R, W, T, C = lay.levels, lay.rows, lay.lanes, lay.tiles, lay.chunks
    F, G, order = lay.feats, lay.gpts, lay.order
    octets = G // 8
    grp, me = lax.axis_index("grp"), lax.axis_index("tile")
    n_grp = lax.axis_size("grp")
    south, north = lax.rem(grp + 1, n_grp), lax.rem(grp + n_grp - 1, n_grp)
    east, west = lax.rem(me + 1, T), lax.rem(me + T - 1, T)
    MESH = pl.DeviceIdType.MESH

    def peer(d):
        return me + sum((1 - 2 * lax.rem(me // (1 << b), 2)) * (1 << b) for b in range(lay.bits) if d >> b & 1)

    loads = [
        pltpu.make_async_copy(temp_in, raw.at[0], in_sem.at[0]),
        pltpu.make_async_copy(humid_in, raw.at[1], in_sem.at[1]),
    ]
    for c in loads:
        c.start()

    barrier = pltpu.get_barrier_semaphore()
    friends = [(grp, peer(d)) for d in [1] + list(range(2, T, 2))]
    friends += [(south, me), (north, me), (grp, east), (grp, west)]
    for f in friends:
        pl.semaphore_signal(barrier, inc=1, device_id=f, device_id_type=MESH)
    pl.semaphore_wait(barrier, len(friends))

    def remote(src, dst, send, recv, to):
        return pltpu.make_async_remote_copy(
            src_ref=src, dst_ref=dst, send_sem=send, recv_sem=recv, device_id=to, device_id_type=MESH
        )

    def stage_copy(b, c):
        return remote(outb[b].at[c], inb[b].at[c], stage_send.at[b, c], stage_recv.at[b, c], (grp, peer(1 << b)))

    def table_at(s, c):
        start = c * W if isinstance(c, int) else pl.multiple_of(c * W, W)
        return tables.at[pl.ds(s * L, L), pl.ds(start, W)]

    def table_copy(d, c):
        return remote(table_at(0, c), table_at(d, c), tab_send.at[d, c], tab_recv.at[d, c], (grp, peer(d)))

    def forward_copy(d, c):
        return remote(table_at(d, c), table_at(d ^ 1, c), tab_send.at[d ^ 1, c], tab_recv.at[d ^ 1, c], (grp, peer(1)))

    def halo_copies(field, k):
        src = [field.at[R - 1], field.at[0], edge_out.at[k, 0], edge_out.at[k, 1]]
        dst = [row_in.at[k, 0], row_in.at[k, 1], edge_in.at[k, 0], edge_in.at[k, 1]]
        to = [(south, me), (north, me), (grp, east), (grp, west)]
        return [remote(src[i], dst[i], halo_send.at[k, i], halo_recv.at[k, i], to[i]) for i in range(4)]

    line = lax.broadcasted_iota(jnp.int32, (W, W), 0)

    def build_onehot(c):
        for r in range(R):
            low = parent_ref[r : r + 1, :] % lay.owned - c * W
            onehot[c * W : (c + 1) * W, r * W : (r + 1) * W] = (line == low).astype(F32).astype(BF16)

    build_onehot(0)

    for i, dst in enumerate((x, h)):
        loads[i].wait()
        for k in range(L):
            level = raw[i, k].astype(F32)
            for j in range(W // 128):
                wide[j, k * R : (k + 1) * R, :] = level[:, j * 128 : (j + 1) * 128]
        for r in range(R):
            for j in range(W // 128):
                dst[r, :, j * 128 : (j + 1) * 128] = wide[j, pl.ds(r, L, stride=R), :].astype(BF16)

    def build_masked(half):
        base = half * lay.block
        slots = order[half * lay.half : (half + 1) * lay.half]
        row = lax.broadcasted_iota(jnp.int32, (16, W), 0)
        want = jnp.full((16, W), -1, jnp.int32)
        for i, s in enumerate(slots):
            want = jnp.where(row // 2 == i, peer(s), want)
        for r in range(R):
            part = slice(r * W, (r + 1) * W)
            owner = jnp.broadcast_to(parent_ref[r : r + 1, :] // lay.owned, (16, W))
            for i, s in enumerate(slots):
                mask = (owner == peer(s)).astype(F32).astype(BF16)
                for v in range(L // 16):
                    src = slice(v * 16, (v + 1) * 16)
                    at = base + i * F + v * 16
                    masked[at : at + 16, part] = x[r, src, :] * mask
                    masked[at + L : at + L + 16, part] = h[r, src, :] * mask
            at = base + lay.half * F
            masked[at : at + 16, part] = (owner == want).astype(F32).astype(BF16)

    def partial(c, half):
        base = half * lay.block
        total = lax.dot_general(
            masked[base : base + lay.block, :],
            onehot[c * W : (c + 1) * W, :],
            (((1,), (1,)), ((), ())),
            preferred_element_type=F32,
        )
        count = total[lay.half * F :]
        high = jnp.floor(count * (1.0 / 32.0))
        row = lax.broadcasted_iota(jnp.int32, (16, W), 0)
        count = jnp.where(row % 2 == 0, high, count - 32.0 * high)
        return total[: lay.half * F], count

    def first_stage(c):
        data, count = partial(c, 1)
        outb[0][c, : lay.half * F] = data.astype(BF16)
        outb[0][c, lay.half * F :] = count.astype(BF16)
        stage_copy(0, c).start()
        data, count = partial(c, 0)
        keep[c, : lay.half * F] = data
        keep[c, lay.half * F :] = count

    def combine(b, c):
        n = T >> b
        size, cnt = n * F, lay.half * F
        stage_copy(b - 1, c).wait_recv()
        count = keep[c, cnt : cnt + 16] + inb[b - 1][c, size : size + 16].astype(F32)
        keep[c, cnt : cnt + 16] = count
        if b == lay.bits:
            keep[c, :size] = keep[c, :size] + inb[b - 1][c, :size].astype(F32)
            return
        cut = size // 2
        outb[b][c, :cut] = (keep[c, cut:size] + inb[b - 1][c, cut:size].astype(F32)).astype(BF16)
        outb[b][c, cut : cut + 16] = pltpu.roll(count, 16 - n, 0).astype(BF16)
        stage_copy(b, c).start()
        keep[c, :cut] = keep[c, :cut] + inb[b - 1][c, :cut].astype(F32)

    build_masked(1)
    build_masked(0)
    first_stage(0)

    lane = lax.broadcasted_iota(jnp.int32, (L, 128), 1)

    def send_halo(field, k):
        right = jnp.zeros((L, 128), F32)
        left = jnp.zeros((L, 128), F32)
        for r in range(R):
            tail = field[r, :, W - 128 :].astype(F32)
            lead = field[r, :, :128].astype(F32)
            right = jnp.where(lane == r, pltpu.roll(tail, (r + 1) % 128, 1), right)
            left = jnp.where(lane == r, pltpu.roll(lead, r, 1) if r else lead, left)
        edge_out[k, 0] = right.astype(BF16)
        edge_out[k, 1] = left.astype(BF16)
        for cp in halo_copies(field, k):
            cp.start()

    def laplace(field, k, r):
        centre = field[r].astype(F32)
        above = (field[r - 1] if r > 0 else row_in[k, 0]).astype(F32)
        below = (field[r + 1] if r < R - 1 else row_in[k, 1]).astype(F32)
        lf = edge_in[k, 0].astype(F32)
        rt = edge_in[k, 1].astype(F32)
        lf = pltpu.roll(lf, 128 - r, 1) if r else lf
        rt = pltpu.roll(rt, 127 - r, 1)
        wst = pltpu.roll(centre, 1, 1)
        est = pltpu.roll(centre, W - 1, 1)
        wst = jnp.concatenate([jnp.where(lane == 0, lf, wst[:, :128]), wst[:, 128:]], 1)
        est = jnp.concatenate([est[:, : W - 128], jnp.where(lane == 127, rt, est[:, W - 128 :])], 1)
        return centre, above + below + wst + est - 4.0 * centre

    for c in range(1, C):
        build_onehot(c)
        first_stage(c)
        if c == 1:
            send_halo(x, 0)
        combine(1, c - 1)
        if c > 1:
            for b in range(2, lay.bits):
                combine(b, c - 2)

    flipped = jnp.transpose(kabs_in[...])
    for k in range(L):
        kabs[k] = jnp.broadcast_to(flipped[:, k : k + 1], (G, 128))
    sub = lax.broadcasted_iota(jnp.int32, (8, 128), 0)
    for p in range(octets):
        for i, ref in enumerate((planck_in, top_in)):
            vec = jnp.zeros((8, 128), F32)
            for j in range(8):
                vec = jnp.where(sub == j, ref[p * 8 + j], vec)
            gvec[i, p] = vec

    combine(1, C - 1)

    group = octets // 2 if octets % 2 == 0 else octets
    scale = L / G

    def column(c, j):
        cols = pl.ds(pl.multiple_of(j * 128, 128), 128)
        cnt_row = lay.half * F
        cnt = keep[c, cnt_row : cnt_row + 8, cols]
        cnt = jnp.maximum(cnt[0:1] * 32.0 + cnt[1:2], 1.0)
        tc = keep[c, 0:L, cols] / cnt
        hc = keep[c, L:F, cols] / cnt
        em = jnp.exp(0.25 * tc)
        emit[0:L, :] = em
        absorb[...] = jnp.exp(0.5 * hc) * (-math.log2(math.e))
        heat[...] = -0.5 * hc
        for k in range(1, L):
            emit[L + k : L + k + 1, :] = emit[k - 1 : k, :] - emit[k : k + 1, :]
        for half in range(octets // group):
            ps = [half * group + p for p in range(group)]
            wt = [gvec[0, p] for p in ps]
            first_em = emit[0:1, :]
            down = [gvec[1, p] - gvec[0, p] * first_em for p in ps]
            before = None
            for i, p in enumerate(ps):
                before = gvec[1, p] if before is None else before + gvec[1, p]
            for k in range(L):
                ab = absorb[k : k + 1, :]
                acc = None
                dk = emit[L + k : L + k + 1, :] if k else None
                for i, p in enumerate(ps):
                    t = jnp.exp2(kabs[k, p * 8 : p * 8 + 8, :] * ab)
                    trans[k, i] = t
                    q = down[i] if k == 0 else down[i] + wt[i] * dk
                    down[i] = t * q
                    acc = down[i] if acc is None else acc + down[i]
                net[k + 1] = acc if half == 0 else net[k + 1] + acc
            last = emit[L - 1 : L, :]
            up = [0.3 * down[i] - (0.7 * wt[i]) * last for i in range(group)]
            for k in range(L - 1, -1, -1):
                acc = None
                dk = emit[L + k + 1 : L + k + 2, :] if k < L - 1 else None
                for i in range(group):
                    q = up[i] if k == L - 1 else up[i] - wt[i] * dk
                    up[i] = trans[k, i] * q
                    acc = up[i] if acc is None else acc + up[i]
                net[k + 1] = net[k + 1] - acc
            after = None
            for i in range(group):
                u0 = up[i] + wt[i] * first_em
                after = u0 if after is None else after + u0
            before = before - after
            net[0] = before if half == 0 else net[0] + before
        for k in range(L):
            row = jnp.sum(net[k] - net[k + 1], axis=0, keepdims=True) * scale
            heat[k : k + 1, :] = heat[k : k + 1, :] + row
        at = pl.multiple_of(c * W + j * 128, 128)
        tables[0:L, pl.ds(at, 128)] = heat[...].astype(BF16)

    evens = list(range(2, T, 2))

    def forward(c):
        for d in evens:
            table_copy(d, c).wait_recv()
            forward_copy(d, c).start()

    def chunk(c, carry):
        combine(lay.bits, c)
        lax.fori_loop(0, W // 128, lambda j, s: (column(c, j), s)[1], 0)
        for d in [1] + evens:
            table_copy(d, c).start()

        @pl.when(c < C - 2)
        def _():
            for b in range(2, lay.bits):
                combine(b, c + 2)

        @pl.when(c > 0)
        def _():
            forward(c - 1)

        return carry

    lax.fori_loop(0, C, chunk, 0)

    forward(C - 1)
    for cp in halo_copies(x, 0):
        cp.wait_recv()
    for c in range(C):
        for d in [1] + [e ^ 1 for e in evens]:
            table_copy(d, c).wait_recv()

    for r in range(R):
        got = jnp.dot(tables[...], onehot[:, r * W : (r + 1) * W], preferred_element_type=F32)
        owner = jnp.broadcast_to(parent_ref[r : r + 1, :] // lay.owned, (L, W))
        picked = got[:L]
        for s in range(1, T):
            picked = jnp.where(owner == peer(s), got[s * L : (s + 1) * L], picked)
        centre, lap = laplace(x, 0, r)
        first = (centre + 0.2 * lap).astype(BF16).astype(F32)
        heat_f = picked + 0.5 * h[r].astype(F32)
        sec[r] = (first + 0.5 * heat_f).astype(BF16)

    send_halo(sec, 1)
    for cp in halo_copies(sec, 1):
        cp.wait_recv()
    for r in range(R):
        centre, lap = laplace(sec, 1, r)
        out_ref[r] = (centre + 0.2 * lap).astype(BF16)

    for c in range(C):
        for b in range(lay.bits):
            stage_copy(b, c).wait_send()
        for d in [1] + evens:
            table_copy(d, c).wait_send()
        for d in evens:
            forward_copy(d, c).wait_send()
    for k, field in enumerate((x, sec)):
        for cp in halo_copies(field, k):
            cp.wait_send()


def fused(temp, humid, parent, kabs, planck, top_flux):
    levels, rows, lanes = temp.shape
    tiles = lax.axis_size("tile")
    gpts = kabs.shape[0]
    lay = Layout(tiles, levels, rows, lanes, gpts)
    octets = gpts // 8
    group = octets // 2 if octets % 2 == 0 else octets
    any_spec = pl.BlockSpec(memory_space=pl.ANY)
    smem = pl.BlockSpec(memory_space=pltpu.SMEM)
    dma = pltpu.SemaphoreType.DMA
    messages = [pltpu.VMEM((lay.chunks, lay.message(b), lanes), BF16) for b in range(lay.bits)]
    out = pl.pallas_call(
        functools.partial(fused_kernel, lay),
        out_shape=jax.ShapeDtypeStruct((rows, levels, lanes), BF16),
        in_specs=[any_spec, any_spec, VSPEC, VSPEC, smem, smem],
        out_specs=VSPEC,
        scratch_shapes=[
            pltpu.VMEM((2, levels, rows, lanes), BF16),
            pltpu.VMEM((lanes // 128, levels * rows, 128), F32),
            pltpu.VMEM((rows, levels, lanes), BF16),
            pltpu.VMEM((rows, levels, lanes), BF16),
            pltpu.VMEM((lay.owned, lay.cells), BF16),
            pltpu.VMEM((2 * lay.block, lay.cells), BF16),
            pltpu.VMEM((lay.chunks, lay.block, lanes), F32),
            *messages,
            *messages,
            pltpu.VMEM((tiles * levels, lay.owned), BF16),
            pltpu.VMEM((levels, gpts, 128), F32),
            pltpu.VMEM((2, octets, 8, 128), F32),
            pltpu.VMEM((levels, group, 8, 128), F32),
            pltpu.VMEM((levels + 1, 8, 128), F32),
            pltpu.VMEM((2 * levels, 128), F32),
            pltpu.VMEM((levels, 128), F32),
            pltpu.VMEM((levels, 128), F32),
            pltpu.VMEM((rows, levels, lanes), BF16),
            pltpu.VMEM((2, 2, levels, 128), BF16),
            pltpu.VMEM((2, 2, levels, 128), BF16),
            pltpu.VMEM((2, 2, levels, lanes), BF16),
            dma((2,)),
            dma((lay.bits, lay.chunks)),
            dma((lay.bits, lay.chunks)),
            dma((tiles, lay.chunks)),
            dma((tiles, lay.chunks)),
            dma((2, 4)),
            dma((2, 4)),
        ],
        compiler_params=pltpu.CompilerParams(
            collective_id=0, has_side_effects=True, vmem_limit_bytes=VMEM_LIMIT
        ),
    )(temp, humid, parent, jnp.transpose(kabs), planck, top_flux)
    return jnp.transpose(out, (1, 0, 2))


def program(*args):
    tiles = lax.axis_size("tile")
    if fused_fits(tiles, *args[0].shape, args[3].shape[0]):
        return fused(*args)
    return on_device(*args)


def solution(mesh):
    return jax.shard_map(
        program,
        mesh=mesh,
        in_specs=(P(None, "grp", "tile"), P(None, "grp", "tile"), P("grp", "tile"), P(), P(), P()),
        out_specs=P(None, "grp", "tile"),
        check_vma=False,
    )
```

```python
import functools
import math

import jax
import jax.numpy as jnp
from jax import lax
from jax.experimental import pallas as pl
from jax.experimental.pallas import tpu as pltpu
from jax.sharding import PartitionSpec as P

F32 = jnp.float32
BF16 = jnp.bfloat16
VMEM_LIMIT = 60 * 1024 * 1024
VSPEC = pl.BlockSpec(memory_space=pltpu.VMEM)


def partial_kernel(chunks, offset_ref, temp_ref, humid_ref, parent_ref, out_ref, onehot, masked):
    rows, levels, lanes = temp_ref.shape
    step = pl.program_id(0)
    owner = 2 * step + offset_ref[0]
    data = 2 * levels * chunks
    row = lax.broadcasted_iota(jnp.int32, (16, lanes), 0)

    @pl.when(step == 0)
    def _():
        lo_iota = lax.broadcasted_iota(jnp.int32, (lanes, lanes), 0)
        for r in range(rows):
            low = parent_ref[r : r + 1, :] % lanes
            onehot[:, r * lanes : (r + 1) * lanes] = (lo_iota == low).astype(F32).astype(BF16)

    for r in range(rows):
        high = jnp.broadcast_to(parent_ref[r : r + 1, :] // lanes, (16, lanes))
        part = slice(r * lanes, (r + 1) * lanes)
        for c in range(chunks):
            mask = (high == owner * chunks + c).astype(F32).astype(BF16)
            for v in range(levels // 16):
                src = slice(v * 16, (v + 1) * 16)
                at = c * 2 * levels + v * 16
                masked[at : at + 16, part] = temp_ref[r, src, :] * mask
                masked[at + levels : at + levels + 16, part] = humid_ref[r, src, :] * mask
        masked[data : data + 16, part] = (high == owner * chunks + row // 2).astype(F32).astype(BF16)
    total = lax.dot_general(
        masked[...], onehot[...], (((1,), (1,)), ((), ())), preferred_element_type=F32
    )
    out_ref[0, :data, :] = total[:data].astype(out_ref.dtype)
    count = total[data:]
    high = jnp.floor(count * (1.0 / 32.0))
    out_ref[0, data:, :] = jnp.where(row % 2 == 0, high, count - 32.0 * high).astype(out_ref.dtype)


def radiate_kernel(levels, feats, recv_ref, kabs_in, planck_ref, top_ref, out_ref, kabs_ref, sums, absorb, emit, trans, net, heat):
    tiles = recv_ref.shape[0]
    lanes = recv_ref.shape[2]
    chunks = recv_ref.shape[1] // feats
    octets = kabs_in.shape[0] // 8
    group = octets // 2 if octets % 2 == 0 else octets
    width = 128
    data = chunks * feats
    for k in range(levels):
        kabs_ref[k] = jnp.broadcast_to(kabs_in[:, k : k + 1], kabs_ref.shape[1:])

    def add(i, carry):
        at = pl.ds(pl.multiple_of(i * 16, 16), 16)
        acc = recv_ref[0, at, :].astype(F32)
        for s in range(1, tiles):
            acc = acc + recv_ref[s, at, :].astype(F32)
        sums[at, :] = acc
        return carry

    lax.fori_loop(0, data // 16 + 1, add, 0)
    for c in range(chunks):
        base = c * feats
        cnt = sums[data + 2 * c : data + 2 * c + 1, :] * 32.0
        cnt = cnt + sums[data + 2 * c + 1 : data + 2 * c + 2, :]
        cnt = jnp.maximum(cnt, 1.0)
        for j in range(lanes // width):
            part = slice(j * width, (j + 1) * width)
            ct = c * (lanes // width) + j
            tc = sums[base : base + levels, part] / cnt[:, part]
            hc = sums[base + levels : base + 2 * levels, part] / cnt[:, part]
            emit[ct] = jnp.exp(0.25 * tc)
            absorb[ct] = jnp.exp(0.5 * hc) * (-math.log2(math.e))
            heat[ct] = -0.5 * hc

    scale = levels / (octets * 8)

    def column(ct, carry):
        for half in range(octets // group):
            gs = [(half * group + p) * 8 for p in range(group)]
            planck = [jnp.broadcast_to(planck_ref[g : g + 8, :], (8, width)) for g in gs]
            down = [jnp.broadcast_to(top_ref[g : g + 8, :], (8, width)) for g in gs]
            if half == 0:
                before = sum(down[1:], down[0])
                net[0] = before
            else:
                net[0] = net[0] + sum(down[1:], down[0])
            for k in range(levels):
                ab = absorb[ct, k : k + 1, :]
                em = emit[ct, k : k + 1, :]
                acc = None
                for p in range(group):
                    t = jnp.exp2(kabs_ref[k, gs[p] : gs[p] + 8, :] * ab)
                    trans[k, p] = t
                    s = planck[p] * em
                    down[p] = s + t * (down[p] - s)
                    acc = down[p] if acc is None else acc + down[p]
                net[k + 1] = acc if half == 0 else net[k + 1] + acc
            up = [0.3 * d for d in down]
            for k in range(levels - 1, -1, -1):
                em = emit[ct, k : k + 1, :]
                acc = None
                for p in range(group):
                    s = planck[p] * em
                    up[p] = s + trans[k, p] * (up[p] - s)
                    acc = up[p] if acc is None else acc + up[p]
                net[k + 1] = net[k + 1] - acc
            net[0] = net[0] - acc
        for k in range(levels):
            row = jnp.sum(net[k] - net[k + 1], axis=0, keepdims=True) * scale
            heat[ct, k : k + 1, :] = heat[ct, k : k + 1, :] + row
        return carry

    lax.fori_loop(0, chunks * lanes // width, column, 0)
    per = lanes // width
    for c in range(chunks):
        for j in range(per):
            out_ref[c * levels : (c + 1) * levels, j * width : (j + 1) * width] = heat[c * per + j].astype(BF16)


def laplace_row(centre, above, below, left, right):
    lanes = centre.shape[1]
    lane = lax.broadcasted_iota(jnp.int32, centre.shape, 1)
    west = jnp.where(lane == 0, left, pltpu.roll(centre, 1, 1))
    east = jnp.where(lane == lanes - 1, right, pltpu.roll(centre, lanes - 1, 1))
    return above + below + west + east - 4.0 * centre


def gather_kernel(levels, table_ref, parent_ref, temp_ref, humid_ref, up_ref, dn_ref, lf_ref, rt_ref, out_ref):
    rows, _, lanes = temp_ref.shape
    tiles = table_ref.shape[0]
    chunks = table_ref.shape[1] // levels
    lo_iota = lax.broadcasted_iota(jnp.int32, (lanes, lanes), 0)
    for r in range(rows):
        low = parent_ref[r : r + 1, :] % lanes
        high = jnp.broadcast_to(parent_ref[r : r + 1, :] // lanes, (levels, lanes))
        onehot = (lo_iota == low).astype(F32).astype(BF16)

        def owner(i, acc):
            span = 4
            got = jnp.dot(
                table_ref[pl.ds(i * span, span)].reshape(span * chunks * levels, lanes),
                onehot,
                preferred_element_type=F32,
            )
            for c in range(span * chunks):
                acc = jnp.where(high == i * span * chunks + c, got[c * levels : (c + 1) * levels], acc)
            return acc

        picked = lax.fori_loop(0, tiles // 4, owner, jnp.zeros((levels, lanes), F32))
        centre = temp_ref[r].astype(F32)
        above = (temp_ref[r - 1] if r > 0 else up_ref[0]).astype(F32)
        below = (temp_ref[r + 1] if r < rows - 1 else dn_ref[0]).astype(F32)
        lap = laplace_row(centre, above, below, lf_ref[:, r : r + 1], rt_ref[:, r : r + 1])
        first = (centre + 0.2 * lap).astype(BF16).astype(F32)
        heat_f = picked + 0.5 * humid_ref[r].astype(F32)
        out_ref[r] = (first + 0.5 * heat_f).astype(BF16)


def laplace_kernel(x_ref, up_ref, dn_ref, lf_ref, rt_ref, out_ref):
    rows = x_ref.shape[0]
    for r in range(rows):
        centre = x_ref[r].astype(F32)
        above = (x_ref[r - 1] if r > 0 else up_ref[0]).astype(F32)
        below = (x_ref[r + 1] if r < rows - 1 else dn_ref[0]).astype(F32)
        lap = laplace_row(centre, above, below, lf_ref[:, r : r + 1], rt_ref[:, r : r + 1])
        out_ref[r] = (centre + 0.2 * lap).astype(BF16)


def halos(x):
    g, t = lax.axis_size("grp"), lax.axis_size("tile")
    ahead = lambda n: [(i, (i + 1) % n) for i in range(n)]
    back = lambda n: [((i + 1) % n, i) for i in range(n)]
    up = lax.ppermute(x[-1:], "grp", ahead(g))
    dn = lax.ppermute(x[:1], "grp", back(g))
    lf = lax.ppermute(jnp.transpose(x[:, :, -1]), "tile", ahead(t)).astype(F32)
    rt = lax.ppermute(jnp.transpose(x[:, :, 0]), "tile", back(t)).astype(F32)
    return up, dn, lf, rt


def on_device(temp, humid, parent, kabs, planck, top_flux):
    levels, rows, lanes = temp.shape
    tiles = lax.axis_size("tile")
    owned = rows * lanes // 4
    chunks = owned // lanes
    feats = 2 * levels
    gpts = kabs.shape[0]
    params = pltpu.CompilerParams(vmem_limit_bytes=VMEM_LIMIT)

    x = jnp.transpose(temp, (1, 0, 2))
    h = jnp.transpose(humid, (1, 0, 2))
    size = chunks * feats + 16
    core = lax.rem(lax.axis_index("tile"), 2)
    half = tiles // 2

    def partial_sums(offset, dtype):
        return pl.pallas_call(
            functools.partial(partial_kernel, chunks),
            out_shape=jax.ShapeDtypeStruct((half, size, lanes), dtype),
            grid=(half,),
            in_specs=[
                pl.BlockSpec(memory_space=pltpu.SMEM),
                pl.BlockSpec((rows, levels, lanes), lambda i: (0, 0, 0)),
                pl.BlockSpec((rows, levels, lanes), lambda i: (0, 0, 0)),
                pl.BlockSpec((rows, lanes), lambda i: (0, 0)),
            ],
            out_specs=pl.BlockSpec((1, size, lanes), lambda i: (i, 0, 0)),
            scratch_shapes=[
                pltpu.VMEM((lanes, rows * lanes), BF16),
                pltpu.VMEM((size, rows * lanes), BF16),
            ],
            compiler_params=params,
            cost_estimate=pl.CostEstimate(
                flops=2 * half * size * rows * lanes * lanes,
                bytes_accessed=4 * half * size * lanes,
                transcendentals=0,
            ),
        )(offset.reshape(1).astype(jnp.int32), x, h, parent)

    theirs = partial_sums(1 - core, BF16)
    given = lax.ppermute(theirs, "tile", [(i, i ^ 1) for i in range(tiles)])
    mine = partial_sums(core, F32)
    partial = (mine + given.astype(F32)).astype(BF16)
    groups = [list(range(c, tiles, 2)) for c in range(2)]
    recv = lax.all_to_all(
        partial, "tile", split_axis=0, concat_axis=0, tiled=True, axis_index_groups=groups
    )

    ctiles = owned // 128
    octets = gpts // 8
    group = octets // 2 if octets % 2 == 0 else octets
    table = pl.pallas_call(
        functools.partial(radiate_kernel, levels, feats),
        out_shape=jax.ShapeDtypeStruct((chunks * levels, lanes), BF16),
        in_specs=[VSPEC] * 4,
        out_specs=VSPEC,
        scratch_shapes=[
            pltpu.VMEM((levels, gpts, 128), F32),
            pltpu.VMEM((size, lanes), F32),
            pltpu.VMEM((ctiles, levels, 128), F32),
            pltpu.VMEM((ctiles, levels, 128), F32),
            pltpu.VMEM((levels, group, 8, 128), F32),
            pltpu.VMEM((levels + 1, 8, 128), F32),
            pltpu.VMEM((ctiles, levels, 128), F32),
        ],
        compiler_params=params,
    )(recv, kabs, planck[:, None], top_flux[:, None])
    tables = lax.all_gather(table, "tile", axis=0)

    second = pl.pallas_call(
        functools.partial(gather_kernel, levels),
        out_shape=jax.ShapeDtypeStruct((rows, levels, lanes), BF16),
        in_specs=[VSPEC] * 8,
        out_specs=VSPEC,
        compiler_params=params,
    )(tables, parent, x, h, *halos(x))
    out = pl.pallas_call(
        laplace_kernel,
        out_shape=jax.ShapeDtypeStruct((rows, levels, lanes), BF16),
        in_specs=[VSPEC] * 5,
        out_specs=VSPEC,
        compiler_params=params,
    )(second, *halos(second))
    return jnp.transpose(out, (1, 0, 2))


class Layout:
    def __init__(self, tiles, levels, rows, lanes, gpts):
        self.tiles, self.levels, self.rows, self.lanes, self.gpts = tiles, levels, rows, lanes, gpts
        self.bits = tiles.bit_length() - 1
        self.owned = rows * lanes // 4
        self.chunks = self.owned // lanes
        self.feats = 2 * levels
        self.per = lanes // 128
        self.pieces = self.chunks * self.per
        self.cells = rows * lanes
        order = [0]
        for b in reversed(range(self.bits)):
            order = order + [s ^ (1 << b) for s in order]
        self.order = order
        self.quarter = tiles // 4
        self.block = self.quarter * self.feats + 16

    def message(self, b):
        return self.block if b < 2 else (self.tiles >> (b + 1)) * self.feats + 16


def fused_fits(tiles, levels, rows, lanes, gpts):
    if tiles & (tiles - 1) or tiles < 4 or tiles > 16 or rows < 16:
        return False
    if levels % 16 or lanes != 256 or rows % 16 or gpts % 8:
        return False
    lay = Layout(tiles, levels, rows, lanes, gpts)
    big = 2 * (4 * lay.block + lay.owned) * lay.cells
    return lay.chunks >= 4 and big <= VMEM_LIMIT // 2


def fused_kernel(lay, *refs):
    (temp_in, humid_in, parent_ref, kabs_in, planck_in, top_in, out_ref,
     raw, wide, x, h, onehot, masked, keep, pair_in, pair_out, *rest) = refs
    inb, rest = rest[: lay.bits - 1], rest[lay.bits - 1 :]
    outb, rest = rest[: lay.bits - 1], rest[lay.bits - 1 :]
    (tables, kabs, gvec, trans, net, emit, absorb, heat, base, sec, edge_out, edge_in, row_in,
     rim_out, rim_in, rimp_out, rimp_in, rimhot,
     in_sem, pair_send, pair_recv, stage_send, stage_recv, tab_send, tab_recv,
     halo_send, halo_recv, rim_send, rim_recv) = rest
    L, R, W, T, C = lay.levels, lay.rows, lay.lanes, lay.tiles, lay.chunks
    N, per = lay.pieces, lay.per
    F, G, Q, B, order = lay.feats, lay.gpts, lay.quarter, lay.block, lay.order
    octets = G // 8
    grp, me = lax.axis_index("grp"), lax.axis_index("tile")
    n_grp = lax.axis_size("grp")
    south, north = lax.rem(grp + 1, n_grp), lax.rem(grp + n_grp - 1, n_grp)
    east, west = lax.rem(me + 1, T), lax.rem(me + T - 1, T)
    MESH = pl.DeviceIdType.MESH

    def peer(d):
        return me + sum((1 - 2 * lax.rem(me // (1 << b), 2)) * (1 << b) for b in range(lay.bits) if d >> b & 1)

    loads = [
        pltpu.make_async_copy(temp_in, raw.at[0], in_sem.at[0]),
        pltpu.make_async_copy(humid_in, raw.at[1], in_sem.at[1]),
    ]
    for c in loads:
        c.start()

    barrier = pltpu.get_barrier_semaphore()
    friends = [(grp, peer(d)) for d in [1] + list(range(2, T, 2))]
    friends += [(south, me), (north, me), (grp, east), (grp, west)]
    for f in friends:
        pl.semaphore_signal(barrier, inc=1, device_id=f, device_id_type=MESH)

    def remote(src, dst, send, recv, to):
        return pltpu.make_async_remote_copy(
            src_ref=src, dst_ref=dst, send_sem=send, recv_sem=recv, device_id=to, device_id_type=MESH
        )

    def pair_copy(i, c):
        return remote(pair_out.at[i, c], pair_in.at[i, c], pair_send.at[i, c], pair_recv.at[i, c], (grp, peer(1)))

    def stage_copy(b, c):
        return remote(
            outb[b - 1].at[c], inb[b - 1].at[c], stage_send.at[b, c], stage_recv.at[b, c], (grp, peer(1 << b))
        )

    def table_at(s, c):
        start = c * 128 if isinstance(c, int) else pl.multiple_of(c * 128, 128)
        return tables.at[pl.ds(s * L, L), pl.ds(start, 128)]

    def table_copy(d, c):
        return remote(table_at(0, c), table_at(d, c), tab_send.at[d, c], tab_recv.at[d, c], (grp, peer(d)))

    def forward_copy(d, c):
        return remote(table_at(d, c), table_at(d ^ 1, c), tab_send.at[d ^ 1, c], tab_recv.at[d ^ 1, c], (grp, peer(1)))

    def row_copies(field, k):
        return [
            remote(field.at[R - 1], row_in.at[k, 0], halo_send.at[k, 0], halo_recv.at[k, 0], (south, me)),
            remote(field.at[0], row_in.at[k, 1], halo_send.at[k, 1], halo_recv.at[k, 1], (north, me)),
        ]

    def edge_copies():
        return [
            remote(edge_out.at[i], edge_in.at[i], halo_send.at[2, i], halo_recv.at[2, i], (grp, to))
            for i, to in enumerate((east, west))
        ]

    def rim_copies():
        return [
            remote(src.at[i], dst.at[i], rim_send.at[n, i], rim_recv.at[n, i], (grp, to))
            for n, (src, dst) in enumerate(((rim_out, rim_in), (rimp_out, rimp_in)))
            for i, to in enumerate((east, west))
        ]

    line = lax.broadcasted_iota(jnp.int32, (W, W), 0)

    def build_onehot(c):
        for r in range(R):
            low = parent_ref[r : r + 1, :] % lay.owned - c * W
            onehot[c * W : (c + 1) * W, r * W : (r + 1) * W] = (line == low).astype(F32).astype(BF16)

    build_onehot(0)

    for i, dst in enumerate((x, h)):
        loads[i].wait()
        for k in range(L):
            level = raw[i, k].astype(F32)
            for j in range(W // 128):
                wide[j, k * R : (k + 1) * R, :] = level[:, j * 128 : (j + 1) * 128]
        for r in range(R):
            for j in range(W // 128):
                dst[r, :, j * 128 : (j + 1) * 128] = wide[j, pl.ds(r, L, stride=R), :].astype(BF16)

    def slots_of(quarter):
        at = {0: 3, 1: 2, 2: 1, 3: 0}[quarter] * Q
        return order[at : at + Q]

    def build_masked(quarter):
        start = quarter * B
        slots = slots_of(quarter)
        row = lax.broadcasted_iota(jnp.int32, (16, W), 0)
        want = jnp.full((16, W), -1, jnp.int32)
        for i, s in enumerate(slots):
            want = jnp.where(row // 2 == i, peer(s), want)
        for r in range(R):
            part = slice(r * W, (r + 1) * W)
            owner = jnp.broadcast_to(parent_ref[r : r + 1, :] // lay.owned, (16, W))
            for i, s in enumerate(slots):
                mask = (owner == peer(s)).astype(F32).astype(BF16)
                for v in range(L // 16):
                    src = slice(v * 16, (v + 1) * 16)
                    at = start + i * F + v * 16
                    masked[at : at + 16, part] = x[r, src, :] * mask
                    masked[at + L : at + L + 16, part] = h[r, src, :] * mask
            at = start + Q * F
            masked[at : at + 16, part] = (owner == want).astype(F32).astype(BF16)

    def partial(c, first, n):
        dots = []
        for base_q in (first, first + 2):
            total = lax.dot_general(
                masked[base_q * B : (base_q + n) * B, :],
                onehot[c * W : (c + 1) * W, :],
                (((1,), (1,)), ((), ())),
                preferred_element_type=F32,
            )
            dots.append(total)
        row = lax.broadcasted_iota(jnp.int32, (16, W), 0)
        for half, total in enumerate(dots):
            for i in range(n):
                data = total[i * B : i * B + Q * F]
                count = total[i * B + Q * F : (i + 1) * B]
                high = jnp.floor(count * (1.0 / 32.0))
                count = jnp.where(row % 2 == 0, high, count - 32.0 * high)
                ref, dtype = ((pair_out, BF16), (keep, F32))[half]
                for j in range(per):
                    cols = slice(j * 128, (j + 1) * 128)
                    ref[first + i, c * per + j, : Q * F] = data[:, cols].astype(dtype)
                    ref[first + i, c * per + j, Q * F :] = count[:, cols].astype(dtype)
        for i in range(n):
            for j in range(per):
                pair_copy(first + i, c * per + j).start()

    def combine(b, c):
        if b == 1:
            pair_copy(0, c).wait_recv()
            outb[0][c] = (keep[0, c] + pair_in[0, c].astype(F32)).astype(BF16)
            stage_copy(1, c).start()
            return
        n = T >> b
        size, cnt = n * F, Q * F
        if b == 2:
            pair_copy(1, c).wait_recv()
            stage_copy(1, c).wait_recv()
            got = lambda part: pair_in[1, c, part].astype(F32) + inb[0][c, part].astype(F32)
            count = keep[1, c, cnt : cnt + 16] + got(slice(cnt, cnt + 16))
        else:
            stage_copy(b - 1, c).wait_recv()
            got = lambda part: inb[b - 2][c, part].astype(F32)
            count = keep[1, c, cnt : cnt + 16] + got(slice(size, size + 16))
        keep[1, c, cnt : cnt + 16] = count
        if b == lay.bits:
            keep[1, c, :size] = keep[1, c, :size] + got(slice(0, size))
            return
        cut = size // 2
        outb[b - 1][c, :cut] = (keep[1, c, cut:size] + got(slice(cut, size))).astype(BF16)
        outb[b - 1][c, cut : cut + 16] = pltpu.roll(count, 16 - n, 0).astype(BF16)
        stage_copy(b, c).start()
        keep[1, c, :cut] = keep[1, c, :cut] + got(slice(0, cut))

    def middle(c):
        for b in range(2, lay.bits):
            combine(b, c)

    lane = lax.broadcasted_iota(jnp.int32, (L, 128), 1)
    spot = lax.broadcasted_iota(jnp.int32, (8, 128), 1)

    def columns(field):
        right = jnp.zeros((L, 128), F32)
        left = jnp.zeros((L, 128), F32)
        for r in range(R):
            tail = field[r, :, W - 128 :].astype(F32)
            lead = field[r, :, :128].astype(F32)
            right = jnp.where(lane == r, pltpu.roll(tail, (r + 1) % 128, 1), right)
            left = jnp.where(lane == r, pltpu.roll(lead, r, 1) if r else lead, left)
        return right, left

    def laplace(field, k, r, lf, rt):
        centre = field[r].astype(F32)
        above = (field[r - 1] if r > 0 else row_in[k, 0]).astype(F32)
        below = (field[r + 1] if r < R - 1 else row_in[k, 1]).astype(F32)
        wst = pltpu.roll(centre, 1, 1)
        est = pltpu.roll(centre, W - 1, 1)
        wst = jnp.concatenate([jnp.where(lane == 0, lf, wst[:, :128]), wst[:, 128:]], 1)
        est = jnp.concatenate([est[:, : W - 128], jnp.where(lane == 127, rt, est[:, W - 128 :])], 1)
        return (centre + 0.2 * (above + below + wst + est - 4.0 * centre)).astype(BF16)

    build_masked(0)
    build_masked(2)
    pl.semaphore_wait(barrier, len(friends))
    partial(0, 0, 1)
    build_masked(1)
    build_masked(3)
    build_onehot(1)
    partial(0, 1, 1)
    for i in range(per):
        combine(1, i)
    sent = per
    for c in range(1, C):
        if c + 1 < C:
            build_onehot(c + 1)
        partial(c, 0, 2)
        if c == 1:
            for i, edge in enumerate(columns(x)):
                edge_out[i] = edge.astype(BF16)
            for cp in row_copies(x, 0) + edge_copies():
                cp.start()
        if c == C - 1:
            middle(0)
        if c > 1:
            combine(1, sent)
            sent += 1

    flipped = jnp.transpose(kabs_in[...])
    for k in range(L):
        kabs[k] = jnp.broadcast_to(flipped[:, k : k + 1], (G, 128))
    sub = lax.broadcasted_iota(jnp.int32, (8, 128), 0)
    for p in range(octets):
        for i, ref in enumerate((planck_in, top_in)):
            vec = jnp.zeros((8, 128), F32)
            for j in range(8):
                vec = jnp.where(sub == j, ref[p * 8 + j], vec)
            gvec[i, p] = vec

    for cp in row_copies(x, 0) + edge_copies():
        cp.wait_recv()
    for r in range(R):
        lf = edge_in[0].astype(F32)
        lf = pltpu.roll(lf, 128 - r, 1) if r else lf
        rt = pltpu.roll(edge_in[1].astype(F32), 127 - r, 1)
        base[r] = laplace(x, 0, r, lf, rt).astype(F32) + 0.25 * h[r].astype(F32)
    for i, edge in enumerate(columns(base)):
        rim_out[i] = edge
    right = jnp.full((8, 128), -1, jnp.int32)
    left = jnp.full((8, 128), -1, jnp.int32)
    for r in range(R):
        line_r = jnp.broadcast_to(parent_ref[r : r + 1, :], (8, W))
        right = jnp.where(spot == r, pltpu.roll(line_r[:, W - 128 :], (r + 1) % 128, 1), right)
        left = jnp.where(spot == r, pltpu.roll(line_r[:, :128], r, 1) if r else line_r[:, :128], left)
    rimp_out[0] = right
    rimp_out[1] = left
    for cp in rim_copies():
        cp.start()
    lead = N // 2
    for i in range(1, lead):
        if i == lead - 1:
            for k in range(sent, N - 1):
                combine(1, k)
            sent = N - 1
        middle(i)
        if sent < N:
            combine(1, sent)
            sent += 1

    group = octets // 2 if octets % 2 == 0 else octets
    scale = L / G

    def column(c):
        cnt = keep[1, c, Q * F : Q * F + 8]
        cnt = jnp.maximum(cnt[0:1] * 32.0 + cnt[1:2], 1.0)
        tc = keep[1, c, 0:L] / cnt
        hc = keep[1, c, L:F] / cnt
        emit[0:L, :] = jnp.exp(0.25 * tc)
        absorb[...] = jnp.exp(0.5 * hc) * (-math.log2(math.e))
        heat[...] = -0.5 * hc
        for k in range(1, L):
            emit[L + k : L + k + 1, :] = emit[k - 1 : k, :] - emit[k : k + 1, :]
        for half in range(octets // group):
            ps = [half * group + p for p in range(group)]
            wt = [gvec[0, p] for p in ps]
            first_em = emit[0:1, :]
            down = [gvec[1, p] - gvec[0, p] * first_em for p in ps]
            before = None
            for p in ps:
                before = gvec[1, p] if before is None else before + gvec[1, p]
            for k in range(L):
                ab = absorb[k : k + 1, :]
                acc = None
                dk = emit[L + k : L + k + 1, :] if k else None
                for i, p in enumerate(ps):
                    t = jnp.exp2(kabs[k, p * 8 : p * 8 + 8, :] * ab)
                    trans[k, i] = t
                    q = down[i] if k == 0 else down[i] + wt[i] * dk
                    down[i] = t * q
                    acc = down[i] if acc is None else acc + down[i]
                net[k + 1] = acc if half == 0 else net[k + 1] + acc
            last = emit[L - 1 : L, :]
            up = [0.3 * down[i] - (0.7 * wt[i]) * last for i in range(group)]
            for k in range(L - 1, -1, -1):
                acc = None
                dk = emit[L + k + 1 : L + k + 2, :] if k < L - 1 else None
                for i in range(group):
                    q = up[i] if k == L - 1 else up[i] - wt[i] * dk
                    up[i] = trans[k, i] * q
                    acc = up[i] if acc is None else acc + up[i]
                net[k + 1] = net[k + 1] - acc
            after = None
            for i in range(group):
                u0 = up[i] + wt[i] * first_em
                after = u0 if after is None else after + u0
            before = before - after
            net[0] = before if half == 0 else net[0] + before
        for k in range(L):
            row = jnp.sum(net[k] - net[k + 1], axis=0, keepdims=True) * scale
            heat[k : k + 1, :] = heat[k : k + 1, :] + row
        at = pl.multiple_of(c * 128, 128)
        tables[0:L, pl.ds(at, 128)] = heat[...].astype(BF16)

    evens = list(range(2, T, 2))

    def forward(c):
        for d in evens:
            table_copy(d, c).wait_recv()
            forward_copy(d, c).start()

    def piece(i, carry):
        combine(lay.bits, i)
        column(i)
        for d in [1] + evens:
            table_copy(d, i).start()

        @pl.when(i < N - lead)
        def _():
            middle(i + lead)

        @pl.when(i >= lag)
        def _():
            forward(i - lag)

        return carry

    lag = N // 2
    lax.fori_loop(0, N, piece, 0)

    arrivals = [1] + [e ^ 1 for e in evens]

    def pick(hot, span, owner):
        got = jnp.dot(tables[:, span], hot, preferred_element_type=F32)
        picked = got[:L]
        for s in range(1, T):
            picked = jnp.where(owner == peer(s), got[s * L : (s + 1) * L], picked)
        return picked

    def gather(r, span):
        owner = jnp.broadcast_to(parent_ref[r : r + 1, :] // lay.owned, (L, W))
        return base[r] + 0.5 * pick(onehot[span, r * W : (r + 1) * W], span, owner)

    early, late = slice(0, (N - lag) * 128), slice((N - lag) * 128, N * 128)
    for i in range(N - lag):
        for d in arrivals:
            table_copy(d, i).wait_recv()
    for r in range(R):
        base[r] = gather(r, early)
        if r % (R // lag) == R // lag - 1:
            forward(N - lag + r // (R // lag))

    for cp in rim_copies():
        cp.wait_recv()
    rimp = jnp.where(spot < R, rimp_in[0], jnp.where(spot < 2 * R, pltpu.roll(rimp_in[1], R, 1), -1))
    low = rimp[0:1, :] % lay.owned
    tall = lax.broadcasted_iota(jnp.int32, (W, 128), 0)
    for c in range(C):
        rimhot[c * W : (c + 1) * W, :] = (tall == low - c * W).astype(F32).astype(BF16)

    for i in range(N - lag, N):
        for d in arrivals:
            table_copy(d, i).wait_recv()
    for r in [0, R - 1] + list(range(1, R - 1)):
        sec[r] = gather(r, late).astype(BF16)
        if r == R - 1:
            for cp in row_copies(sec, 1):
                cp.start()
    owner = jnp.broadcast_to(rimp[0:1, :] // lay.owned, (L, 128))
    rim = jnp.where(lane < R, rim_in[0], pltpu.roll(rim_in[1], R, 1))
    rim = (rim + 0.5 * pick(rimhot[...], slice(0, C * W), owner)).astype(BF16).astype(F32)

    for cp in row_copies(sec, 1):
        cp.wait_recv()
    for r in range(R):
        lf = pltpu.roll(rim, 128 - r, 1) if r else rim
        rt = pltpu.roll(rim, 127 - R - r, 1)
        out_ref[r] = laplace(sec, 1, r, lf, rt)

    for c in range(N):
        for i in range(2):
            pair_copy(i, c).wait_send()
        for b in range(1, lay.bits):
            stage_copy(b, c).wait_send()
        for d in [1] + evens:
            table_copy(d, c).wait_send()
        for d in evens:
            forward_copy(d, c).wait_send()
    for cp in row_copies(x, 0) + edge_copies() + rim_copies() + row_copies(sec, 1):
        cp.wait_send()


def fused(temp, humid, parent, kabs, planck, top_flux):
    levels, rows, lanes = temp.shape
    tiles = lax.axis_size("tile")
    gpts = kabs.shape[0]
    lay = Layout(tiles, levels, rows, lanes, gpts)
    octets = gpts // 8
    group = octets // 2 if octets % 2 == 0 else octets
    any_spec = pl.BlockSpec(memory_space=pl.ANY)
    smem = pl.BlockSpec(memory_space=pltpu.SMEM)
    dma = pltpu.SemaphoreType.DMA
    messages = [pltpu.VMEM((lay.pieces, lay.message(b), 128), BF16) for b in range(1, lay.bits)]
    out = pl.pallas_call(
        functools.partial(fused_kernel, lay),
        out_shape=jax.ShapeDtypeStruct((rows, levels, lanes), BF16),
        in_specs=[any_spec, any_spec, VSPEC, VSPEC, smem, smem],
        out_specs=VSPEC,
        scratch_shapes=[
            pltpu.VMEM((2, levels, rows, lanes), BF16),
            pltpu.VMEM((lanes // 128, levels * rows, 128), F32),
            pltpu.VMEM((rows, levels, lanes), BF16),
            pltpu.VMEM((rows, levels, lanes), BF16),
            pltpu.VMEM((lay.owned, lay.cells), BF16),
            pltpu.VMEM((4 * lay.block, lay.cells), BF16),
            pltpu.VMEM((2, lay.pieces, lay.block, 128), F32),
            pltpu.VMEM((2, lay.pieces, lay.block, 128), BF16),
            pltpu.VMEM((2, lay.pieces, lay.block, 128), BF16),
            *messages,
            *messages,
            pltpu.VMEM((tiles * levels, lay.owned), BF16),
            pltpu.VMEM((levels, gpts, 128), F32),
            pltpu.VMEM((2, octets, 8, 128), F32),
            pltpu.VMEM((levels, group, 8, 128), F32),
            pltpu.VMEM((levels + 1, 8, 128), F32),
            pltpu.VMEM((2 * levels, 128), F32),
            pltpu.VMEM((levels, 128), F32),
            pltpu.VMEM((levels, 128), F32),
            pltpu.VMEM((rows, levels, lanes), F32),
            pltpu.VMEM((rows, levels, lanes), BF16),
            pltpu.VMEM((2, levels, 128), BF16),
            pltpu.VMEM((2, levels, 128), BF16),
            pltpu.VMEM((2, 2, levels, lanes), BF16),
            pltpu.VMEM((2, levels, 128), F32),
            pltpu.VMEM((2, levels, 128), F32),
            pltpu.VMEM((2, 8, 128), jnp.int32),
            pltpu.VMEM((2, 8, 128), jnp.int32),
            pltpu.VMEM((lay.owned, 128), BF16),
            dma((2,)),
            dma((2, lay.pieces)),
            dma((2, lay.pieces)),
            dma((lay.bits, lay.pieces)),
            dma((lay.bits, lay.pieces)),
            dma((tiles, lay.pieces)),
            dma((tiles, lay.pieces)),
            dma((3, 2)),
            dma((3, 2)),
            dma((2, 2)),
            dma((2, 2)),
        ],
        compiler_params=pltpu.CompilerParams(
            collective_id=0, has_side_effects=True, vmem_limit_bytes=VMEM_LIMIT
        ),
    )(temp, humid, parent, jnp.transpose(kabs), planck, top_flux)
    return jnp.transpose(out, (1, 0, 2))


def program(*args):
    tiles = lax.axis_size("tile")
    if fused_fits(tiles, *args[0].shape, args[3].shape[0]):
        return fused(*args)
    return on_device(*args)


def solution(mesh):
    return jax.shard_map(
        program,
        mesh=mesh,
        in_specs=(P(None, "grp", "tile"), P(None, "grp", "tile"), P("grp", "tile"), P(), P(), P()),
        out_specs=P(None, "grp", "tile"),
        check_vma=False,
    )
```

```python
import functools
import math

import jax
import jax.numpy as jnp
from jax import lax
from jax.experimental import pallas as pl
from jax.experimental.pallas import tpu as pltpu
from jax.sharding import PartitionSpec as P

F32 = jnp.float32
BF16 = jnp.bfloat16
VMEM_LIMIT = 60 * 1024 * 1024
VSPEC = pl.BlockSpec(memory_space=pltpu.VMEM)


def partial_kernel(chunks, offset_ref, temp_ref, humid_ref, parent_ref, out_ref, onehot, masked):
    rows, levels, lanes = temp_ref.shape
    step = pl.program_id(0)
    owner = 2 * step + offset_ref[0]
    data = 2 * levels * chunks
    row = lax.broadcasted_iota(jnp.int32, (16, lanes), 0)

    @pl.when(step == 0)
    def _():
        lo_iota = lax.broadcasted_iota(jnp.int32, (lanes, lanes), 0)
        for r in range(rows):
            low = parent_ref[r : r + 1, :] % lanes
            onehot[:, r * lanes : (r + 1) * lanes] = (lo_iota == low).astype(F32).astype(BF16)

    for r in range(rows):
        high = jnp.broadcast_to(parent_ref[r : r + 1, :] // lanes, (16, lanes))
        part = slice(r * lanes, (r + 1) * lanes)
        for c in range(chunks):
            mask = (high == owner * chunks + c).astype(F32).astype(BF16)
            for v in range(levels // 16):
                src = slice(v * 16, (v + 1) * 16)
                at = c * 2 * levels + v * 16
                masked[at : at + 16, part] = temp_ref[r, src, :] * mask
                masked[at + levels : at + levels + 16, part] = humid_ref[r, src, :] * mask
        masked[data : data + 16, part] = (high == owner * chunks + row // 2).astype(F32).astype(BF16)
    total = lax.dot_general(
        masked[...], onehot[...], (((1,), (1,)), ((), ())), preferred_element_type=F32
    )
    out_ref[0, :data, :] = total[:data].astype(out_ref.dtype)
    count = total[data:]
    high = jnp.floor(count * (1.0 / 32.0))
    out_ref[0, data:, :] = jnp.where(row % 2 == 0, high, count - 32.0 * high).astype(out_ref.dtype)


def radiate_kernel(levels, feats, recv_ref, kabs_in, planck_ref, top_ref, out_ref, kabs_ref, sums, absorb, emit, trans, net, heat):
    tiles = recv_ref.shape[0]
    lanes = recv_ref.shape[2]
    chunks = recv_ref.shape[1] // feats
    octets = kabs_in.shape[0] // 8
    group = octets // 2 if octets % 2 == 0 else octets
    width = 128
    data = chunks * feats
    for k in range(levels):
        kabs_ref[k] = jnp.broadcast_to(kabs_in[:, k : k + 1], kabs_ref.shape[1:])

    def add(i, carry):
        at = pl.ds(pl.multiple_of(i * 16, 16), 16)
        acc = recv_ref[0, at, :].astype(F32)
        for s in range(1, tiles):
            acc = acc + recv_ref[s, at, :].astype(F32)
        sums[at, :] = acc
        return carry

    lax.fori_loop(0, data // 16 + 1, add, 0)
    for c in range(chunks):
        base = c * feats
        cnt = sums[data + 2 * c : data + 2 * c + 1, :] * 32.0
        cnt = cnt + sums[data + 2 * c + 1 : data + 2 * c + 2, :]
        cnt = jnp.maximum(cnt, 1.0)
        for j in range(lanes // width):
            part = slice(j * width, (j + 1) * width)
            ct = c * (lanes // width) + j
            tc = sums[base : base + levels, part] / cnt[:, part]
            hc = sums[base + levels : base + 2 * levels, part] / cnt[:, part]
            emit[ct] = jnp.exp(0.25 * tc)
            absorb[ct] = jnp.exp(0.5 * hc) * (-math.log2(math.e))
            heat[ct] = -0.5 * hc

    scale = levels / (octets * 8)

    def column(ct, carry):
        for half in range(octets // group):
            gs = [(half * group + p) * 8 for p in range(group)]
            planck = [jnp.broadcast_to(planck_ref[g : g + 8, :], (8, width)) for g in gs]
            down = [jnp.broadcast_to(top_ref[g : g + 8, :], (8, width)) for g in gs]
            if half == 0:
                before = sum(down[1:], down[0])
                net[0] = before
            else:
                net[0] = net[0] + sum(down[1:], down[0])
            for k in range(levels):
                ab = absorb[ct, k : k + 1, :]
                em = emit[ct, k : k + 1, :]
                acc = None
                for p in range(group):
                    t = jnp.exp2(kabs_ref[k, gs[p] : gs[p] + 8, :] * ab)
                    trans[k, p] = t
                    s = planck[p] * em
                    down[p] = s + t * (down[p] - s)
                    acc = down[p] if acc is None else acc + down[p]
                net[k + 1] = acc if half == 0 else net[k + 1] + acc
            up = [0.3 * d for d in down]
            for k in range(levels - 1, -1, -1):
                em = emit[ct, k : k + 1, :]
                acc = None
                for p in range(group):
                    s = planck[p] * em
                    up[p] = s + trans[k, p] * (up[p] - s)
                    acc = up[p] if acc is None else acc + up[p]
                net[k + 1] = net[k + 1] - acc
            net[0] = net[0] - acc
        for k in range(levels):
            row = jnp.sum(net[k] - net[k + 1], axis=0, keepdims=True) * scale
            heat[ct, k : k + 1, :] = heat[ct, k : k + 1, :] + row
        return carry

    lax.fori_loop(0, chunks * lanes // width, column, 0)
    per = lanes // width
    for c in range(chunks):
        for j in range(per):
            out_ref[c * levels : (c + 1) * levels, j * width : (j + 1) * width] = heat[c * per + j].astype(BF16)


def laplace_row(centre, above, below, left, right):
    lanes = centre.shape[1]
    lane = lax.broadcasted_iota(jnp.int32, centre.shape, 1)
    west = jnp.where(lane == 0, left, pltpu.roll(centre, 1, 1))
    east = jnp.where(lane == lanes - 1, right, pltpu.roll(centre, lanes - 1, 1))
    return above + below + west + east - 4.0 * centre


def gather_kernel(levels, table_ref, parent_ref, temp_ref, humid_ref, up_ref, dn_ref, lf_ref, rt_ref, out_ref):
    rows, _, lanes = temp_ref.shape
    tiles = table_ref.shape[0]
    chunks = table_ref.shape[1] // levels
    lo_iota = lax.broadcasted_iota(jnp.int32, (lanes, lanes), 0)
    for r in range(rows):
        low = parent_ref[r : r + 1, :] % lanes
        high = jnp.broadcast_to(parent_ref[r : r + 1, :] // lanes, (levels, lanes))
        onehot = (lo_iota == low).astype(F32).astype(BF16)

        def owner(i, acc):
            span = 4
            got = jnp.dot(
                table_ref[pl.ds(i * span, span)].reshape(span * chunks * levels, lanes),
                onehot,
                preferred_element_type=F32,
            )
            for c in range(span * chunks):
                acc = jnp.where(high == i * span * chunks + c, got[c * levels : (c + 1) * levels], acc)
            return acc

        picked = lax.fori_loop(0, tiles // 4, owner, jnp.zeros((levels, lanes), F32))
        centre = temp_ref[r].astype(F32)
        above = (temp_ref[r - 1] if r > 0 else up_ref[0]).astype(F32)
        below = (temp_ref[r + 1] if r < rows - 1 else dn_ref[0]).astype(F32)
        lap = laplace_row(centre, above, below, lf_ref[:, r : r + 1], rt_ref[:, r : r + 1])
        first = (centre + 0.2 * lap).astype(BF16).astype(F32)
        heat_f = picked + 0.5 * humid_ref[r].astype(F32)
        out_ref[r] = (first + 0.5 * heat_f).astype(BF16)


def laplace_kernel(x_ref, up_ref, dn_ref, lf_ref, rt_ref, out_ref):
    rows = x_ref.shape[0]
    for r in range(rows):
        centre = x_ref[r].astype(F32)
        above = (x_ref[r - 1] if r > 0 else up_ref[0]).astype(F32)
        below = (x_ref[r + 1] if r < rows - 1 else dn_ref[0]).astype(F32)
        lap = laplace_row(centre, above, below, lf_ref[:, r : r + 1], rt_ref[:, r : r + 1])
        out_ref[r] = (centre + 0.2 * lap).astype(BF16)


def halos(x):
    g, t = lax.axis_size("grp"), lax.axis_size("tile")
    ahead = lambda n: [(i, (i + 1) % n) for i in range(n)]
    back = lambda n: [((i + 1) % n, i) for i in range(n)]
    up = lax.ppermute(x[-1:], "grp", ahead(g))
    dn = lax.ppermute(x[:1], "grp", back(g))
    lf = lax.ppermute(jnp.transpose(x[:, :, -1]), "tile", ahead(t)).astype(F32)
    rt = lax.ppermute(jnp.transpose(x[:, :, 0]), "tile", back(t)).astype(F32)
    return up, dn, lf, rt


def on_device(temp, humid, parent, kabs, planck, top_flux):
    levels, rows, lanes = temp.shape
    tiles = lax.axis_size("tile")
    owned = rows * lanes // 4
    chunks = owned // lanes
    feats = 2 * levels
    gpts = kabs.shape[0]
    params = pltpu.CompilerParams(vmem_limit_bytes=VMEM_LIMIT)

    x = jnp.transpose(temp, (1, 0, 2))
    h = jnp.transpose(humid, (1, 0, 2))
    size = chunks * feats + 16
    core = lax.rem(lax.axis_index("tile"), 2)
    half = tiles // 2

    def partial_sums(offset, dtype):
        return pl.pallas_call(
            functools.partial(partial_kernel, chunks),
            out_shape=jax.ShapeDtypeStruct((half, size, lanes), dtype),
            grid=(half,),
            in_specs=[
                pl.BlockSpec(memory_space=pltpu.SMEM),
                pl.BlockSpec((rows, levels, lanes), lambda i: (0, 0, 0)),
                pl.BlockSpec((rows, levels, lanes), lambda i: (0, 0, 0)),
                pl.BlockSpec((rows, lanes), lambda i: (0, 0)),
            ],
            out_specs=pl.BlockSpec((1, size, lanes), lambda i: (i, 0, 0)),
            scratch_shapes=[
                pltpu.VMEM((lanes, rows * lanes), BF16),
                pltpu.VMEM((size, rows * lanes), BF16),
            ],
            compiler_params=params,
            cost_estimate=pl.CostEstimate(
                flops=2 * half * size * rows * lanes * lanes,
                bytes_accessed=4 * half * size * lanes,
                transcendentals=0,
            ),
        )(offset.reshape(1).astype(jnp.int32), x, h, parent)

    theirs = partial_sums(1 - core, BF16)
    given = lax.ppermute(theirs, "tile", [(i, i ^ 1) for i in range(tiles)])
    mine = partial_sums(core, F32)
    partial = (mine + given.astype(F32)).astype(BF16)
    groups = [list(range(c, tiles, 2)) for c in range(2)]
    recv = lax.all_to_all(
        partial, "tile", split_axis=0, concat_axis=0, tiled=True, axis_index_groups=groups
    )

    ctiles = owned // 128
    octets = gpts // 8
    group = octets // 2 if octets % 2 == 0 else octets
    table = pl.pallas_call(
        functools.partial(radiate_kernel, levels, feats),
        out_shape=jax.ShapeDtypeStruct((chunks * levels, lanes), BF16),
        in_specs=[VSPEC] * 4,
        out_specs=VSPEC,
        scratch_shapes=[
            pltpu.VMEM((levels, gpts, 128), F32),
            pltpu.VMEM((size, lanes), F32),
            pltpu.VMEM((ctiles, levels, 128), F32),
            pltpu.VMEM((ctiles, levels, 128), F32),
            pltpu.VMEM((levels, group, 8, 128), F32),
            pltpu.VMEM((levels + 1, 8, 128), F32),
            pltpu.VMEM((ctiles, levels, 128), F32),
        ],
        compiler_params=params,
    )(recv, kabs, planck[:, None], top_flux[:, None])
    tables = lax.all_gather(table, "tile", axis=0)

    second = pl.pallas_call(
        functools.partial(gather_kernel, levels),
        out_shape=jax.ShapeDtypeStruct((rows, levels, lanes), BF16),
        in_specs=[VSPEC] * 8,
        out_specs=VSPEC,
        compiler_params=params,
    )(tables, parent, x, h, *halos(x))
    out = pl.pallas_call(
        laplace_kernel,
        out_shape=jax.ShapeDtypeStruct((rows, levels, lanes), BF16),
        in_specs=[VSPEC] * 5,
        out_specs=VSPEC,
        compiler_params=params,
    )(second, *halos(second))
    return jnp.transpose(out, (1, 0, 2))


class Layout:
    def __init__(self, tiles, levels, rows, lanes, gpts):
        self.tiles, self.levels, self.rows, self.lanes, self.gpts = tiles, levels, rows, lanes, gpts
        self.bits = tiles.bit_length() - 1
        self.owned = rows * lanes // 4
        self.chunks = self.owned // lanes
        self.feats = 2 * levels
        self.per = lanes // 128
        self.pieces = self.chunks * self.per
        self.cells = rows * lanes
        order = [0]
        for b in reversed(range(self.bits)):
            order = order + [s ^ (1 << b) for s in order]
        self.order = order
        self.quarter = tiles // 4
        self.block = self.quarter * self.feats + 16

    def message(self, b):
        return self.block if b < 2 else (self.tiles >> (b + 1)) * self.feats + 16


def fused_fits(tiles, levels, rows, lanes, gpts):
    if tiles & (tiles - 1) or tiles < 4 or tiles > 16 or rows < 16:
        return False
    if levels % 16 or lanes != 256 or rows % 16 or gpts % 8:
        return False
    lay = Layout(tiles, levels, rows, lanes, gpts)
    big = 2 * (4 * lay.block + lay.owned) * lay.cells
    return lay.chunks >= 4 and big <= VMEM_LIMIT // 2


def fused_kernel(lay, *refs):
    (temp_in, humid_in, parent_ref, kabs_in, planck_in, top_in, out_ref,
     raw, wide, x, h, onehot, masked, keep, pair_in, pair_out, *rest) = refs
    inb, rest = rest[: lay.bits - 1], rest[lay.bits - 1 :]
    outb, rest = rest[: lay.bits - 1], rest[lay.bits - 1 :]
    (tables, kabs, gvec, trans, net, emit, absorb, heat, base, sec, edge_out, edge_in, row_in,
     rim_out, rim_in, rimp_out, rimp_in, rimhot,
     in_sem, pair_send, pair_recv, stage_send, stage_recv, tab_send, tab_recv,
     halo_send, halo_recv, rim_send, rim_recv) = rest
    L, R, W, T, C = lay.levels, lay.rows, lay.lanes, lay.tiles, lay.chunks
    N, per = lay.pieces, lay.per
    F, G, Q, B, order = lay.feats, lay.gpts, lay.quarter, lay.block, lay.order
    octets = G // 8
    grp, me = lax.axis_index("grp"), lax.axis_index("tile")
    n_grp = lax.axis_size("grp")
    south, north = lax.rem(grp + 1, n_grp), lax.rem(grp + n_grp - 1, n_grp)
    east, west = lax.rem(me + 1, T), lax.rem(me + T - 1, T)
    MESH = pl.DeviceIdType.MESH

    def peer(d):
        return me + sum((1 - 2 * lax.rem(me // (1 << b), 2)) * (1 << b) for b in range(lay.bits) if d >> b & 1)

    loads = [
        pltpu.make_async_copy(temp_in, raw.at[0], in_sem.at[0]),
        pltpu.make_async_copy(humid_in, raw.at[1], in_sem.at[1]),
    ]
    for c in loads:
        c.start()

    barrier = pltpu.get_barrier_semaphore()
    friends = [(grp, peer(d)) for d in [1] + list(range(2, T, 2))]
    friends += [(south, me), (north, me), (grp, east), (grp, west)]
    for f in friends:
        pl.semaphore_signal(barrier, inc=1, device_id=f, device_id_type=MESH)

    def remote(src, dst, send, recv, to):
        return pltpu.make_async_remote_copy(
            src_ref=src, dst_ref=dst, send_sem=send, recv_sem=recv, device_id=to, device_id_type=MESH
        )

    def pair_copy(i, c):
        return remote(pair_out.at[i, c], pair_in.at[i, c], pair_send.at[i, c], pair_recv.at[i, c], (grp, peer(1)))

    def stage_copy(b, c):
        return remote(
            outb[b - 1].at[c], inb[b - 1].at[c], stage_send.at[b, c], stage_recv.at[b, c], (grp, peer(1 << b))
        )

    def table_at(s, c):
        start = c * 128 if isinstance(c, int) else pl.multiple_of(c * 128, 128)
        return tables.at[pl.ds(s * L, L), pl.ds(start, 128)]

    def table_copy(d, c):
        return remote(table_at(0, c), table_at(d, c), tab_send.at[d, c], tab_recv.at[d, c], (grp, peer(d)))

    def forward_copy(d, c):
        return remote(table_at(d, c), table_at(d ^ 1, c), tab_send.at[d ^ 1, c], tab_recv.at[d ^ 1, c], (grp, peer(1)))

    def row_copies(field, k):
        return [
            remote(field.at[R - 1], row_in.at[k, 0], halo_send.at[k, 0], halo_recv.at[k, 0], (south, me)),
            remote(field.at[0], row_in.at[k, 1], halo_send.at[k, 1], halo_recv.at[k, 1], (north, me)),
        ]

    def edge_copies():
        return [
            remote(edge_out.at[i], edge_in.at[i], halo_send.at[2, i], halo_recv.at[2, i], (grp, to))
            for i, to in enumerate((east, west))
        ]

    def rim_copies():
        return [
            remote(src.at[i], dst.at[i], rim_send.at[n, i], rim_recv.at[n, i], (grp, to))
            for n, (src, dst) in enumerate(((rim_out, rim_in), (rimp_out, rimp_in)))
            for i, to in enumerate((east, west))
        ]

    line = lax.broadcasted_iota(jnp.int32, (W, W), 0)

    def build_onehot(c):
        def row(r, carry):
            low = parent_ref[pl.ds(r, 1), :] % lay.owned - c * W
            at = pl.ds(pl.multiple_of(r * W, W), W)
            onehot[c * W : (c + 1) * W, at] = (line == low).astype(F32).astype(BF16)
            return carry

        lax.fori_loop(0, R, row, 0)

    build_onehot(0)

    for i, dst in enumerate((x, h)):
        loads[i].wait()
        for k in range(L):
            level = raw[i, k].astype(F32)
            for j in range(W // 128):
                wide[j, k * R : (k + 1) * R, :] = level[:, j * 128 : (j + 1) * 128]
        for r in range(R):
            for j in range(W // 128):
                dst[r, :, j * 128 : (j + 1) * 128] = wide[j, pl.ds(r, L, stride=R), :].astype(BF16)

    def slots_of(quarter):
        at = {0: 3, 1: 2, 2: 1, 3: 0}[quarter] * Q
        return order[at : at + Q]

    def build_masked(quarter):
        start = quarter * B
        slots = slots_of(quarter)
        row = lax.broadcasted_iota(jnp.int32, (16, W), 0)
        want = jnp.full((16, W), -1, jnp.int32)
        for i, s in enumerate(slots):
            want = jnp.where(row // 2 == i, peer(s), want)
        for r in range(R):
            part = slice(r * W, (r + 1) * W)
            owner = jnp.broadcast_to(parent_ref[r : r + 1, :] // lay.owned, (16, W))
            for i, s in enumerate(slots):
                mask = (owner == peer(s)).astype(F32).astype(BF16)
                for v in range(L // 16):
                    src = slice(v * 16, (v + 1) * 16)
                    at = start + i * F + v * 16
                    masked[at : at + 16, part] = x[r, src, :] * mask
                    masked[at + L : at + L + 16, part] = h[r, src, :] * mask
            at = start + Q * F
            masked[at : at + 16, part] = (owner == want).astype(F32).astype(BF16)

    def partial(c, first, n):
        dots = []
        for base_q in (first, first + 2):
            total = lax.dot_general(
                masked[base_q * B : (base_q + n) * B, :],
                onehot[c * W : (c + 1) * W, :],
                (((1,), (1,)), ((), ())),
                preferred_element_type=F32,
            )
            dots.append(total)
        row = lax.broadcasted_iota(jnp.int32, (16, W), 0)
        for half, total in enumerate(dots):
            for i in range(n):
                data = total[i * B : i * B + Q * F]
                count = total[i * B + Q * F : (i + 1) * B]
                high = jnp.floor(count * (1.0 / 32.0))
                count = jnp.where(row % 2 == 0, high, count - 32.0 * high)
                ref, dtype = ((pair_out, BF16), (keep, F32))[half]
                for j in range(per):
                    cols = slice(j * 128, (j + 1) * 128)
                    ref[first + i, c * per + j, : Q * F] = data[:, cols].astype(dtype)
                    ref[first + i, c * per + j, Q * F :] = count[:, cols].astype(dtype)
        for i in range(n):
            for j in range(per):
                pair_copy(first + i, c * per + j).start()

    def combine(b, c):
        if b == 1:
            pair_copy(0, c).wait_recv()
            outb[0][c] = (keep[0, c] + pair_in[0, c].astype(F32)).astype(BF16)
            stage_copy(1, c).start()
            return
        n = T >> b
        size, cnt = n * F, Q * F
        if b == 2:
            pair_copy(1, c).wait_recv()
            stage_copy(1, c).wait_recv()
            got = lambda part: pair_in[1, c, part].astype(F32) + inb[0][c, part].astype(F32)
            count = keep[1, c, cnt : cnt + 16] + got(slice(cnt, cnt + 16))
        else:
            stage_copy(b - 1, c).wait_recv()
            got = lambda part: inb[b - 2][c, part].astype(F32)
            count = keep[1, c, cnt : cnt + 16] + got(slice(size, size + 16))
        keep[1, c, cnt : cnt + 16] = count
        if b == lay.bits:
            keep[1, c, :size] = keep[1, c, :size] + got(slice(0, size))
            return
        cut = size // 2
        outb[b - 1][c, :cut] = (keep[1, c, cut:size] + got(slice(cut, size))).astype(BF16)
        outb[b - 1][c, cut : cut + 16] = pltpu.roll(count, 16 - n, 0).astype(BF16)
        stage_copy(b, c).start()
        keep[1, c, :cut] = keep[1, c, :cut] + got(slice(0, cut))

    def middle(c):
        for b in range(2, lay.bits):
            combine(b, c)

    lane = lax.broadcasted_iota(jnp.int32, (L, 128), 1)
    spot = lax.broadcasted_iota(jnp.int32, (8, 128), 1)

    def columns(field):
        right = jnp.zeros((L, 128), F32)
        left = jnp.zeros((L, 128), F32)
        for r in range(R):
            tail = field[r, :, W - 128 :].astype(F32)
            lead = field[r, :, :128].astype(F32)
            right = jnp.where(lane == r, pltpu.roll(tail, (r + 1) % 128, 1), right)
            left = jnp.where(lane == r, pltpu.roll(lead, r, 1) if r else lead, left)
        return right, left

    def laplace(field, k, r, lf, rt):
        centre = field[r].astype(F32)
        above = (field[r - 1] if r > 0 else row_in[k, 0]).astype(F32)
        below = (field[r + 1] if r < R - 1 else row_in[k, 1]).astype(F32)
        wst = pltpu.roll(centre, 1, 1)
        est = pltpu.roll(centre, W - 1, 1)
        wst = jnp.concatenate([jnp.where(lane == 0, lf, wst[:, :128]), wst[:, 128:]], 1)
        est = jnp.concatenate([est[:, : W - 128], jnp.where(lane == 127, rt, est[:, W - 128 :])], 1)
        return (centre + 0.2 * (above + below + wst + est - 4.0 * centre)).astype(BF16)

    build_masked(0)
    build_masked(2)
    pl.semaphore_wait(barrier, len(friends))
    partial(0, 0, 1)
    build_masked(1)
    build_masked(3)
    build_onehot(1)
    partial(0, 1, 1)
    for i in range(per):
        combine(1, i)
    for c in range(1, C):
        if c + 1 < C:
            build_onehot(c + 1)
        partial(c, 0, 2)
        if c == 1:
            for i, edge in enumerate(columns(x)):
                edge_out[i] = edge.astype(BF16)
            for cp in row_copies(x, 0) + edge_copies():
                cp.start()
        if c > 1:
            for i in range((c - 1) * per, c * per):
                combine(1, i)
            middle(c - 2)

    flipped = jnp.transpose(kabs_in[...])
    for k in range(L):
        kabs[k] = jnp.broadcast_to(flipped[:, k : k + 1], (G, 128))
    sub = lax.broadcasted_iota(jnp.int32, (8, 128), 0)
    for p in range(octets):
        for i, ref in enumerate((planck_in, top_in)):
            vec = jnp.zeros((8, 128), F32)
            for j in range(8):
                vec = jnp.where(sub == j, ref[p * 8 + j], vec)
            gvec[i, p] = vec
    for i in range(N - per, N):
        combine(1, i)
    middle(C - 2)

    for cp in row_copies(x, 0) + edge_copies():
        cp.wait_recv()
    for r in range(R):
        lf = edge_in[0].astype(F32)
        lf = pltpu.roll(lf, 128 - r, 1) if r else lf
        rt = pltpu.roll(edge_in[1].astype(F32), 127 - r, 1)
        base[r] = laplace(x, 0, r, lf, rt).astype(F32) + 0.25 * h[r].astype(F32)
    for i, edge in enumerate(columns(base)):
        rim_out[i] = edge
    right = jnp.full((8, 128), -1, jnp.int32)
    left = jnp.full((8, 128), -1, jnp.int32)
    for r in range(R):
        line_r = jnp.broadcast_to(parent_ref[r : r + 1, :], (8, W))
        right = jnp.where(spot == r, pltpu.roll(line_r[:, W - 128 :], (r + 1) % 128, 1), right)
        left = jnp.where(spot == r, pltpu.roll(line_r[:, :128], r, 1) if r else line_r[:, :128], left)
    rimp_out[0] = right
    rimp_out[1] = left
    for cp in rim_copies():
        cp.start()
    lead = N // 2
    for i in range(C - 1, lead):
        middle(i)

    group = octets // 2 if octets % 2 == 0 else octets
    scale = L / G

    def column(c):
        cnt = keep[1, c, Q * F : Q * F + 8]
        cnt = jnp.maximum(cnt[0:1] * 32.0 + cnt[1:2], 1.0)
        tc = keep[1, c, 0:L] / cnt
        hc = keep[1, c, L:F] / cnt
        emit[0:L, :] = jnp.exp(0.25 * tc)
        absorb[...] = jnp.exp(0.5 * hc) * (-math.log2(math.e))
        heat[...] = -0.5 * hc
        for k in range(1, L):
            emit[L + k : L + k + 1, :] = emit[k - 1 : k, :] - emit[k : k + 1, :]
        for half in range(octets // group):
            ps = [half * group + p for p in range(group)]
            wt = [gvec[0, p] for p in ps]
            first_em = emit[0:1, :]
            down = [gvec[1, p] - gvec[0, p] * first_em for p in ps]
            before = None
            for p in ps:
                before = gvec[1, p] if before is None else before + gvec[1, p]
            for k in range(L):
                ab = absorb[k : k + 1, :]
                acc = None
                dk = emit[L + k : L + k + 1, :] if k else None
                for i, p in enumerate(ps):
                    t = jnp.exp2(kabs[k, p * 8 : p * 8 + 8, :] * ab)
                    trans[k, i] = t
                    q = down[i] if k == 0 else down[i] + wt[i] * dk
                    down[i] = t * q
                    acc = down[i] if acc is None else acc + down[i]
                net[k + 1] = acc if half == 0 else net[k + 1] + acc
            last = emit[L - 1 : L, :]
            up = [0.3 * down[i] - (0.7 * wt[i]) * last for i in range(group)]
            for k in range(L - 1, -1, -1):
                acc = None
                dk = emit[L + k + 1 : L + k + 2, :] if k < L - 1 else None
                for i in range(group):
                    q = up[i] if k == L - 1 else up[i] - wt[i] * dk
                    up[i] = trans[k, i] * q
                    acc = up[i] if acc is None else acc + up[i]
                net[k + 1] = net[k + 1] - acc
            after = None
            for i in range(group):
                u0 = up[i] + wt[i] * first_em
                after = u0 if after is None else after + u0
            before = before - after
            net[0] = before if half == 0 else net[0] + before
        for k in range(L):
            row = jnp.sum(net[k] - net[k + 1], axis=0, keepdims=True) * scale
            heat[k : k + 1, :] = heat[k : k + 1, :] + row
        at = pl.multiple_of(c * 128, 128)
        tables[0:L, pl.ds(at, 128)] = heat[...].astype(BF16)

    evens = list(range(2, T, 2))

    def forward(c):
        for d in evens:
            table_copy(d, c).wait_recv()
            forward_copy(d, c).start()

    def piece(i, carry):
        combine(lay.bits, i)

        @pl.when(i < N - lead)
        def _():
            middle(i + lead)

        column(i)
        for d in [1] + evens:
            table_copy(d, i).start()

        @pl.when(i >= lag)
        def _():
            forward(i - lag)

        return carry

    lag = N // 2
    lax.fori_loop(0, N, piece, 0)

    arrivals = [1] + [e ^ 1 for e in evens]

    def pick(hot, span, owner):
        got = jnp.dot(tables[:, span], hot, preferred_element_type=F32)
        picked = got[:L]
        for s in range(1, T):
            picked = jnp.where(owner == peer(s), got[s * L : (s + 1) * L], picked)
        return picked

    def gather(r, span):
        owner = jnp.broadcast_to(parent_ref[r : r + 1, :] // lay.owned, (L, W))
        return base[r] + 0.5 * pick(onehot[span, r * W : (r + 1) * W], span, owner)

    early, late = slice(0, (N - lag) * 128), slice((N - lag) * 128, N * 128)
    for i in range(N - lag):
        for d in arrivals:
            table_copy(d, i).wait_recv()
    for r in range(R):
        base[r] = gather(r, early)
        if r % (R // lag) == R // lag - 1:
            forward(N - lag + r // (R // lag))

    for cp in rim_copies():
        cp.wait_recv()
    rimp = jnp.where(spot < R, rimp_in[0], jnp.where(spot < 2 * R, pltpu.roll(rimp_in[1], R, 1), -1))
    low = rimp[0:1, :] % lay.owned
    tall = lax.broadcasted_iota(jnp.int32, (W, 128), 0)
    for c in range(C):
        rimhot[c * W : (c + 1) * W, :] = (tall == low - c * W).astype(F32).astype(BF16)

    for i in range(N - lag, N):
        for d in arrivals:
            table_copy(d, i).wait_recv()
    for r in [0, R - 1] + list(range(1, R - 1)):
        sec[r] = gather(r, late).astype(BF16)
        if r == R - 1:
            for cp in row_copies(sec, 1):
                cp.start()
    owner = jnp.broadcast_to(rimp[0:1, :] // lay.owned, (L, 128))
    rim = jnp.where(lane < R, rim_in[0], pltpu.roll(rim_in[1], R, 1))
    rim = (rim + 0.5 * pick(rimhot[...], slice(0, C * W), owner)).astype(BF16).astype(F32)

    for cp in row_copies(sec, 1):
        cp.wait_recv()
    for r in range(R):
        lf = pltpu.roll(rim, 128 - r, 1) if r else rim
        rt = pltpu.roll(rim, 127 - R - r, 1)
        out_ref[r] = laplace(sec, 1, r, lf, rt)

    for c in range(N):
        for i in range(2):
            pair_copy(i, c).wait_send()
        for b in range(1, lay.bits):
            stage_copy(b, c).wait_send()
        for d in [1] + evens:
            table_copy(d, c).wait_send()
        for d in evens:
            forward_copy(d, c).wait_send()
    for cp in row_copies(x, 0) + edge_copies() + rim_copies() + row_copies(sec, 1):
        cp.wait_send()


def fused(temp, humid, parent, kabs, planck, top_flux):
    levels, rows, lanes = temp.shape
    tiles = lax.axis_size("tile")
    gpts = kabs.shape[0]
    lay = Layout(tiles, levels, rows, lanes, gpts)
    octets = gpts // 8
    group = octets // 2 if octets % 2 == 0 else octets
    any_spec = pl.BlockSpec(memory_space=pl.ANY)
    smem = pl.BlockSpec(memory_space=pltpu.SMEM)
    dma = pltpu.SemaphoreType.DMA
    messages = [pltpu.VMEM((lay.pieces, lay.message(b), 128), BF16) for b in range(1, lay.bits)]
    out = pl.pallas_call(
        functools.partial(fused_kernel, lay),
        out_shape=jax.ShapeDtypeStruct((rows, levels, lanes), BF16),
        in_specs=[any_spec, any_spec, VSPEC, VSPEC, smem, smem],
        out_specs=VSPEC,
        scratch_shapes=[
            pltpu.VMEM((2, levels, rows, lanes), BF16),
            pltpu.VMEM((lanes // 128, levels * rows, 128), F32),
            pltpu.VMEM((rows, levels, lanes), BF16),
            pltpu.VMEM((rows, levels, lanes), BF16),
            pltpu.VMEM((lay.owned, lay.cells), BF16),
            pltpu.VMEM((4 * lay.block, lay.cells), BF16),
            pltpu.VMEM((2, lay.pieces, lay.block, 128), F32),
            pltpu.VMEM((2, lay.pieces, lay.block, 128), BF16),
            pltpu.VMEM((2, lay.pieces, lay.block, 128), BF16),
            *messages,
            *messages,
            pltpu.VMEM((tiles * levels, lay.owned), BF16),
            pltpu.VMEM((levels, gpts, 128), F32),
            pltpu.VMEM((2, octets, 8, 128), F32),
            pltpu.VMEM((levels, group, 8, 128), F32),
            pltpu.VMEM((levels + 1, 8, 128), F32),
            pltpu.VMEM((2 * levels, 128), F32),
            pltpu.VMEM((levels, 128), F32),
            pltpu.VMEM((levels, 128), F32),
            pltpu.VMEM((rows, levels, lanes), F32),
            pltpu.VMEM((rows, levels, lanes), BF16),
            pltpu.VMEM((2, levels, 128), BF16),
            pltpu.VMEM((2, levels, 128), BF16),
            pltpu.VMEM((2, 2, levels, lanes), BF16),
            pltpu.VMEM((2, levels, 128), F32),
            pltpu.VMEM((2, levels, 128), F32),
            pltpu.VMEM((2, 8, 128), jnp.int32),
            pltpu.VMEM((2, 8, 128), jnp.int32),
            pltpu.VMEM((lay.owned, 128), BF16),
            dma((2,)),
            dma((2, lay.pieces)),
            dma((2, lay.pieces)),
            dma((lay.bits, lay.pieces)),
            dma((lay.bits, lay.pieces)),
            dma((tiles, lay.pieces)),
            dma((tiles, lay.pieces)),
            dma((3, 2)),
            dma((3, 2)),
            dma((2, 2)),
            dma((2, 2)),
        ],
        compiler_params=pltpu.CompilerParams(
            collective_id=0, has_side_effects=True, vmem_limit_bytes=VMEM_LIMIT
        ),
    )(temp, humid, parent, jnp.transpose(kabs), planck, top_flux)
    return jnp.transpose(out, (1, 0, 2))


def program(*args):
    tiles = lax.axis_size("tile")
    if fused_fits(tiles, *args[0].shape, args[3].shape[0]):
        return fused(*args)
    return on_device(*args)


def solution(mesh):
    return jax.shard_map(
        program,
        mesh=mesh,
        in_specs=(P(None, "grp", "tile"), P(None, "grp", "tile"), P("grp", "tile"), P(), P(), P()),
        out_specs=P(None, "grp", "tile"),
        check_vma=False,
    )
```
